768 devices in a mesh: group: 16 (over z_lo, x), fsdp: 48 (over z_hi, y, core).
Axes of the slice: x: 4, y: 8, z: 12 (z_hi: 3, z_lo: 4; z = z_hi * 4 + z_lo), core: 2. Of those that a mesh axis runs over, the one named last changes fastest.
Arguments:
- hidden_input_slots: bfloat16 [4096, 8192], P('group'), may hold values from -6 to 6
- base_weight: bfloat16 [8192, 14784], P('group', 'fsdp'), may hold values from -0.0625 to 0.0625
- adapter_a: bfloat16 [8192, 64], P('group'), may hold values from -0.0625 to 0.0625
- adapter_up_matrix: bfloat16 [64, 14784], P(None, 'fsdp'), may hold values from -0.75 to 0.75
- upstream: bfloat16 [4096, 14784], P('group', 'fsdp'), may hold values from -6 to 6
- logp_new: float32 [16, 16, 16], P('group'), may hold values from -2 to -0.5
- logp_old: float32 [16, 16, 16], P('group'), may hold values from -2 to -0.5
- rewards: float32 [16, 16], P('group'), may hold values from -1.35 to 2.35
- comp_lengths: int32 [16, 16], P('group'), may hold values from 1 to 16, 160 in all within a row
- assignment: int32 [16, 16], P('group'), may hold values from 0 to 15, each once within a row
Outputs:
- projection_output: bfloat16 [4096, 14784], P('group', 'fsdp')
- gradient_down_adapter: float32 [8192, 64], P('group')
- gradient_up_adapter: float32 [64, 14784], P('group', 'fsdp')
- loss_parts: float32 [16], P('group')
The draws below stay inside these ranges and needn't reach their ends.
Inputs may be any that keep to these rules, and one draw needn't show every extreme that they name: `comp_lengths`: every generator group has a completion of exactly 16 tokens. `assignment`: each generator group assigns exactly one completion to each trainer group.
All inputs are finite; a program needn't handle non-finite values.
Results may differ from the reference program's by a relative error of at most 0.0049.
Values may be sent and summed in bfloat16 or wider, within the bound.
A program may use at most 64 MiB of HBM per device.

```python
import math
import jax
import jax.numpy as jnp
import numpy as np
from jax import lax

D = 8192
FFW = 14784
R = 64
LEN = 16
COMP = 16
TOKENS = 4096
PROMPTS = 16
N_GROUP = 16


def draw_rewards(key, part):
    prompts = (jnp.arange(N_GROUP * N_GROUP, dtype=jnp.int32) // COMP).reshape(N_GROUP, N_GROUP)
    levels = jax.random.randint(jax.random.fold_in(key, 12), (PROMPTS,), 0, 5).astype(jnp.float32) / 4.0
    success = levels[prompts]
    uniform_draw = jax.random.uniform(jax.random.fold_in(key, 13), (N_GROUP, N_GROUP), dtype=jnp.float32)
    correct = (uniform_draw < success).astype(jnp.float32)
    row_scale = 1.0 + 2.0 * jnp.arange(N_GROUP).astype(jnp.float32)[:, None] / max(N_GROUP - 1, 1)
    noise = jax.random.truncated_normal(jax.random.fold_in(key, 14), -3.0, 3.0, (N_GROUP, N_GROUP), dtype=jnp.float32)
    return correct + 0.15 * row_scale * noise


def block_levels(key, shape, cuts, low, largest):
    gain, own = 1.0, jax.random.fold_in(key, 6)
    for position, blocks in cuts:
        heights = jnp.exp(jax.random.uniform(jax.random.fold_in(own, position), (blocks,), jnp.float32, low / len(cuts), largest / len(cuts)))
        gain = gain * jnp.repeat(heights, shape[position] // blocks).reshape([-1 if axis == position else 1 for axis in range(len(shape))])
    return gain


def profile(amount, total, bound, lean):
    loads = [(1 << 20) // math.isqrt(rank ** lean) + 1 for rank in range(2, amount + 1)]
    surplus, holding = total - bound - (amount - 1), [1] * (amount - 1)
    while surplus > 0:
        candidates = [i for i in range(amount - 1) if holding[i] < bound]
        pool, left = sum([loads[i] for i in candidates]), surplus
        for i in candidates:
            more = min(bound - holding[i], max(1, left * loads[i] // pool), surplus)
            holding[i] = holding[i] + more
            surplus = surplus - more
    return np.array([bound] + holding)


def uneven(key, count, total, most, slope):
    if count == 2:
        one = jax.random.randint(key, (), max(1, total - most), min(most, total - 1) + 1)
        return jnp.stack([one, total - one])
    sizes = jnp.asarray(profile(count, total, most, slope), jnp.int32)
    pairs = (count - 1) // 2
    giver, receiver = sizes[1:1 + 2 * pairs:2], sizes[2:2 + 2 * pairs:2]
    room = jnp.minimum(giver - 1, most - receiver)
    moved = jax.random.randint(jax.random.fold_in(key, 1), (pairs,), 0, 1 << 20) % (room + 1)
    sizes = sizes.at[1:1 + 2 * pairs:2].set(giver - moved).at[2:2 + 2 * pairs:2].set(receiver + moved)
    return sizes[jax.random.permutation(jax.random.fold_in(key, 2), count)]


def centred(rng, extent, scale, most, cuts=(), kind=jnp.bfloat16):
    loudness = block_levels(rng, extent, cuts, -0.22, 0.18) if cuts else 1.0
    array = jax.random.normal(rng, extent, jnp.float32) * scale * loudness
    return jnp.minimum(jnp.maximum(array, -most), most).astype(kind)


def setup_inputs(seed: int = 0) -> dict:
    keys = jax.random.split(jax.random.key(seed), 11)
    return {
        "hidden_input_slots": centred(keys[0], (TOKENS, D), 1.0, 6.0, ((0, 16),)),
        "base_weight": centred(keys[1], (D, FFW), D ** -0.5, 0.0625, ((0, 16), (1, 48))),
        "adapter_a": centred(keys[2], (D, R), D ** -0.5, 0.0625, ((0, 16),)),
        "adapter_up_matrix": centred(keys[3], (R, FFW), R ** -0.5, 0.75, ((1, 48),)),
        "upstream": centred(keys[4], (TOKENS, FFW), 1.0, 6.0, ((0, 16), (1, 48))),
        "logp_new": jnp.clip(-2.0 + 1.5 * jax.random.uniform(keys[5], (N_GROUP, N_GROUP, LEN), jnp.float32) ** block_levels(keys[5], (N_GROUP, N_GROUP, LEN), ((0, 16),), -0.2, 0.2), -2.0, -0.5),
        "logp_old": jnp.clip(-2.0 + 1.5 * jax.random.uniform(keys[6], (N_GROUP, N_GROUP, LEN), jnp.float32) ** block_levels(keys[6], (N_GROUP, N_GROUP, LEN), ((0, 16),), -0.2, 0.2), -2.0, -0.5),
        "rewards": draw_rewards(jax.random.fold_in(keys[10], 71), 0),
        "comp_lengths": jax.vmap(lambda own: uneven(own, N_GROUP, N_GROUP * LEN * 5 // 8, LEN, 1))(jax.random.split(keys[8], N_GROUP)).reshape((N_GROUP, N_GROUP)).astype(jnp.int32),
        "assignment": jax.vmap(lambda own: jax.random.permutation(own, N_GROUP))(jax.random.split(keys[9], N_GROUP)).reshape((N_GROUP, N_GROUP)).astype(jnp.int32),
    }


ADAPTER_SCALING = 0.25
SPREAD_FLOOR = 0.16

def prompt_table(prompt_row, count):
    return (prompt_row[:, None] == jnp.arange(count, dtype=jnp.int32)[None, :]).astype(jnp.float32)

def advantages(reward_row, onehot, reward_sums, reward_squares):
    reward_mean = reward_sums / COMP
    reward_var = reward_squares / COMP - reward_mean * reward_mean
    spread = jnp.sqrt(jnp.maximum(reward_var, SPREAD_FLOOR))
    centre = jnp.dot(onehot, reward_mean, precision=lax.Precision.HIGHEST)
    scaled = jnp.dot(onehot, spread, precision=lax.Precision.HIGHEST)
    return (reward_row - centre) / scaled

def reference(hidden_input_slots, base_weight, adapter_a, adapter_up_matrix, upstream, logp_new, logp_old, rewards, comp_lengths, assignment):
    flat_rewards = rewards.reshape(-1)
    prompt_row = (jnp.arange(N_GROUP * N_GROUP, dtype=jnp.int32) // COMP).astype(jnp.int32)
    onehot = prompt_table(prompt_row, PROMPTS)
    reward_sums = jnp.dot(flat_rewards, onehot, precision=lax.Precision.HIGHEST)
    reward_squares = jnp.dot(flat_rewards * flat_rewards, onehot, precision=lax.Precision.HIGHEST)
    advantage = advantages(flat_rewards, onehot, reward_sums, reward_squares).reshape(N_GROUP, N_GROUP)
    handover = (assignment[:, None, :] == jnp.arange(N_GROUP, dtype=jnp.int32)[None, :, None]).astype(jnp.float32)
    recv_old = jnp.einsum('jtk,jki->tji', handover, logp_old, precision=lax.Precision.HIGHEST)
    recv_adv = jnp.einsum('jtk,jk->tj', handover, advantage, precision=lax.Precision.HIGHEST)
    recv_len = jnp.einsum('jtk,jk->tj', handover, comp_lengths.astype(jnp.float32), precision=lax.Precision.HIGHEST)
    positions = jnp.arange(LEN).astype(jnp.float32)
    live_mask = positions[None, None, :] < recv_len[:, :, None]
    prob_ratio = jnp.exp(logp_new - recv_old)
    token_coef = jnp.where(live_mask, -(recv_adv[:, :, None] * prob_ratio) / (recv_len[:, :, None] * COMP), 0.0)
    loss_parts = lax.optimization_barrier(jnp.sum(token_coef, axis=(1, 2)))
    output_gradient = (token_coef.reshape(TOKENS, 1) * upstream.astype(jnp.float32)).astype(jnp.bfloat16)
    reduced_rank_product = jnp.dot(hidden_input_slots, adapter_a, preferred_element_type=jnp.float32).astype(jnp.bfloat16)
    frozen_base_term = jnp.dot(hidden_input_slots, base_weight, preferred_element_type=jnp.float32)
    projection_output = (frozen_base_term + ADAPTER_SCALING * jnp.dot(reduced_rank_product, adapter_up_matrix, preferred_element_type=jnp.float32)).astype(jnp.bfloat16)
    gradient_up_adapter = ADAPTER_SCALING * jnp.dot(reduced_rank_product.T, output_gradient, preferred_element_type=jnp.float32)
    backward_lowrank = jnp.dot(output_gradient, adapter_up_matrix.T, preferred_element_type=jnp.float32).astype(jnp.bfloat16)
    gradient_down_adapter = ADAPTER_SCALING * jnp.dot(hidden_input_slots.T, backward_lowrank, preferred_element_type=jnp.float32)
    return (projection_output, gradient_down_adapter, gradient_up_adapter, loss_parts)
```

```python
import jax
import jax.numpy as jnp
from jax import lax
from jax.experimental import pallas as pl
from jax.experimental.pallas import tpu as pltpu
from jax.sharding import PartitionSpec as P

COMP = 16
ADAPTER_SCALING = 0.25
SPREAD_FLOOR = 0.16

N = 16
SIDE = 4
M = 16
TOP = 3
MESH = pl.DeviceIdType.MESH
ROWS = 320
HALF = 160
F32 = jnp.float32
BF16 = jnp.bfloat16


def dot_nn(a, b):
    return lax.dot_general(a, b, (((1,), (0,)), ((), ())), preferred_element_type=F32)


def dot_nt(a, b):
    return lax.dot_general(a, b, (((1,), (1,)), ((), ())), preferred_element_type=F32)


def kernel(
    x_hbm, w_ref, a_ref, up_ref, ups_ref, new_ref, old_ref, rew_ref, len_ref, asg_ref,
    proj_ref, gdown_ref, gup_ref, loss_ref,
    xv, wg, acc, up_p, upt, og, row, tab, hs, hr, ag_a, red, rs, zx, ag, gus, gur, gds, gdr, gda,
    x_sem, h_s, h_r, a_s, a_r, zs, xs, fs, w_r, r_s, r_r, z_s, z_r, g_s, g_r, u_s, u_r, d_s, d_r, e_s, e_r,
):
    g = lax.axis_index("group")
    f = lax.axis_index("fsdp")
    z, x = lax.div(g, SIDE), lax.rem(g, SIDE)
    zh, i = lax.div(f, M), lax.rem(f, M)
    a, b = lax.div(i, SIDE), lax.rem(i, SIDE)
    hidden = w_ref.shape[0]
    cols = w_ref.shape[1]

    def copy(src, dst, ss, rr, tg, tf):
        return pltpu.make_async_remote_copy(
            src_ref=src, dst_ref=dst, send_sem=ss, recv_sem=rr,
            device_id=(tg, tf), device_id_type=MESH,
        )

    def each(fn, count=N):
        def body(d, carry):
            fn(d)
            return carry

        lax.fori_loop(1, count, body, 0)

    def group_to(d):
        return lax.rem(g + d, N)

    def group_from(d):
        return lax.rem(g + N - d, N)

    def side_to(d):
        return lax.rem(i + d, M)

    def side_from(d):
        return lax.rem(i + M - d, M)

    def top_to(d):
        return lax.rem(zh + d, TOP)

    def top_from(d):
        return lax.rem(zh + TOP - d, TOP)

    def gx(src, dst, ss, rr, d):
        return copy(src.at[group_to(d)], dst.at[g], ss.at[d], rr.at[d], group_to(d), f)

    def gx_in(src, dst, ss, rr, d):
        j = group_from(d)
        return copy(src.at[j], dst.at[j], ss.at[d], rr.at[d], j, f)

    def sx(src, dst, ss, rr, d):
        return copy(src.at[side_to(d)], dst.at[i], ss.at[d], rr.at[d], g, zh * M + side_to(d))

    def sx_in(src, dst, ss, rr, d):
        j = side_from(d)
        return copy(src.at[j], dst.at[j], ss.at[d], rr.at[d], g, zh * M + j)

    def sg(buf, ss, rr, d):
        return copy(buf.at[i], buf.at[i], ss.at[d], rr.at[d], g, zh * M + side_to(d))

    def sg_in(buf, ss, rr, d):
        j = side_from(d)
        return copy(buf.at[j], buf.at[j], ss.at[d], rr.at[d], g, zh * M + j)

    def tx(d):
        return copy(zx.at[zh], zx.at[zh], z_s.at[d], z_r.at[d], g, top_to(d) * M + i)

    def tx_in(d):
        j = top_from(d)
        return copy(zx.at[j], zx.at[j], z_s.at[d], z_r.at[d], g, j * M + i)

    x_copy = pltpu.make_async_copy(x_hbm, xv, x_sem)
    x_copy.start()

    barrier = pltpu.get_barrier_semaphore()

    def greet(d):
        pl.semaphore_signal(barrier, inc=1, device_id=(group_to(d), f), device_id_type=MESH)
        pl.semaphore_signal(barrier, inc=1, device_id=(g, zh * M + side_to(d)), device_id_type=MESH)

    each(greet)
    each(
        lambda d: pl.semaphore_signal(
            barrier, inc=1, device_id=(g, top_to(d) * M + i), device_id_type=MESH
        ),
        TOP,
    )

    wg[g, HALF + 144 : ROWS, :] = jnp.zeros((16, cols), BF16)
    wg[g, 0:hidden, :] = w_ref[...]

    rewards = rew_ref[...]
    mean = jnp.sum(rewards, axis=1, keepdims=True) / COMP
    var = jnp.sum(rewards * rewards, axis=1, keepdims=True) / COMP - mean * mean
    spread = jnp.sqrt(jnp.maximum(var, SPREAD_FLOOR))
    advantage = (rewards - mean) / spread
    dest = asg_ref[...] == lax.broadcasted_iota(jnp.int32, (N, N), 0)
    lengths = len_ref[...].astype(F32)
    old = old_ref[0]
    sent_old = jnp.zeros((N, N), F32)
    for k in range(N):
        sent_old = jnp.where(dest[:, k : k + 1], old[k : k + 1, :], sent_old)
    sent_adv = jnp.sum(jnp.where(dest, advantage, 0.0), axis=1, keepdims=True)
    sent_len = jnp.sum(jnp.where(dest, lengths, 0.0), axis=1, keepdims=True)
    hs[...] = jnp.zeros(hs.shape, F32)
    for at, value in enumerate((sent_old, sent_adv, sent_len)):
        tab[...] = jnp.zeros(tab.shape, F32)
        tab[:, 0:N] = jnp.broadcast_to(value, (N, N))
        rolled = pltpu.roll(tab[...], g * N, axis=1)
        for t in range(N):
            hs[t, at : at + 1, :] = rolled[t : t + 1, :]
    hr[g] = hs[g]
    for j in range(N):
        row[0:1, j * N : (j + 1) * N] = new_ref[0, j : j + 1, :]

    up_p[...] = jnp.zeros(up_p.shape, BF16)
    up_p[:, 0:hidden] = up_ref[...]
    upt[...] = up_p[...].astype(F32).T.astype(BF16)
    og[...] = jnp.zeros(og.shape, BF16)

    pl.semaphore_wait(barrier, 2 * (N - 1) + TOP - 1)

    each(lambda d: gx(hs, hr, h_s, h_r, d).start())

    quarter = pl.ds(pl.multiple_of(b * 128, 128), 128)

    def ax(d):
        return copy(
            a_ref.at[:, quarter], ag_a.at[z], a_s.at[d], a_r.at[z], group_to(d), f
        )

    @pl.when(x == a)
    def _():
        ag_a[z] = a_ref[:, quarter]
        each(lambda d: ax(d).start())

    right = z * SIDE + lax.rem(x + 1, SIDE)
    left = z * SIDE + lax.rem(x + SIDE - 1, SIDE)

    def part(s, h):
        return wg.at[s, pl.ds(h * HALF, HALF), :]

    def wx(s, h, sem, tg):
        return copy(part(s, h), part(s, h), sem, w_r.at[s, h], tg, f)

    def arrive(s, h):
        wx(s, h, fs.at[0, 0], g).wait_recv()

    near = [z, z + 1 - 2 * lax.rem(z, 2), 2 - lax.div(z, 2), 3 - 3 * lax.div(z, 2)]
    inner = (z == 1) | (z == 2)
    beyond = [None, 3 - z, 3 * (z - 1), 3 * (z - 1)]

    def z_first(go):
        for h in (0, 1):

            @pl.when(z < SIDE - 1)
            def _():
                go(wx(g, h, zs.at[0, h], g + SIDE))

            @pl.when(z > 0)
            def _():
                go(wx(g, h, zs.at[4, h], g - SIDE))

    def z_next(k, go):
        @pl.when(inner)
        def _():
            for h in (0, 1):
                go(wx(near[k] * SIDE + x, h, zs.at[k, h], beyond[k] * SIDE + x))

    def x_send(k, go):
        s = near[k] * SIDE + x
        go(wx(s, 0, xs.at[k, 0, 0], right))
        go(wx(s, 1, xs.at[k, 1, 1], left))
        go(wx(s, 1, xs.at[k, 0, 1], right))
        go(wx(s, 0, xs.at[k, 1, 0], left))

    def shard(k, off):
        return near[k] * SIDE + lax.rem(x + off, SIDE)

    def x_pass(k, go):
        go(wx(shard(k, 3), 0, fs.at[k, 0], right))
        go(wx(shard(k, 1), 1, fs.at[k, 1], left))

    def start(c):
        c.start()

    def done(c):
        c.wait_send()

    def pass_on(k):
        arrive(shard(k, 3), 0)
        arrive(shard(k, 1), 1)
        x_pass(k, start)

    def take(k):
        s = near[k] * SIDE + x
        arrive(s, 0)
        arrive(s, 1)
        z_next(k, start)

    def multiply(s, first=False):
        piece = dot_nt(wg[s], xv[:, pl.ds(pl.multiple_of(s * cols, cols), cols)])
        if first:
            acc[...] = piece
        else:
            acc[...] += piece

    def finish(k):
        arrive(shard(k, 3), 1)
        multiply(shard(k, 3))
        arrive(shard(k, 1), 0)
        multiply(shard(k, 1))
        arrive(shard(k, 2), 0)
        arrive(shard(k, 2), 1)
        multiply(shard(k, 2))

    z_first(start)
    x_send(0, start)

    each(lambda d: gx_in(hs, hr, h_s, h_r, d).wait_recv())
    got = hr[0]
    for j in range(1, N):
        got = got + hr[j]
    recv_old, recv_adv, recv_len = got[0:1, :], got[1:2, :], got[2:3, :]
    position = lax.rem(lax.broadcasted_iota(jnp.int32, (1, N * N), 1), N).astype(F32)
    ratio = jnp.exp(row[0:1, :] - recv_old)
    coef = jnp.where(position < recv_len, -(recv_adv * ratio) / (recv_len * COMP), 0.0)
    loss_ref[...] = jnp.sum(coef, axis=1, keepdims=True)
    og[0:hidden, :] = (coef * ups_ref[...].astype(F32)).astype(BF16)
    back = dot_nn(up_p[...], og[...])
    for p in range(8):
        red[8 + p] = back[p * 8 : (p + 1) * 8, :]

    pass_on(0)

    for q in range(SIDE):

        @pl.when((x != a) | (z != q))
        def _():
            copy(
                a_ref.at[:, quarter], ag_a.at[q], a_s.at[0], a_r.at[q], g, f
            ).wait_recv()

    x_copy.wait()
    low = jnp.zeros((64, N * N), F32)
    for q in range(SIDE):
        at = (q * SIDE + a) * cols + b * 128
        low = low + dot_nt(ag_a[q], xv[:, pl.ds(pl.multiple_of(at, 128), 128)])
    for p in range(8):
        red[p] = low[p * 8 : (p + 1) * 8, :]
    rs[i] = red[i]
    each(lambda d: sx(red, rs, r_s, r_r, d).start())

    take(1)
    x_send(1, start)
    take(2)
    x_send(2, start)
    multiply(g, first=True)

    each(lambda d: sx_in(red, rs, r_s, r_r, d).wait_recv())
    total = rs[0]
    for j in range(1, M):
        total = total + rs[j]
    ag[i] = total.astype(BF16).astype(F32)

    @pl.when(i >= 8)
    def _():
        zx[zh] = total
        each(lambda d: tx(d).start(), TOP)

    pass_on(1)
    take(3)

    @pl.when(i >= 8)
    def _():
        each(lambda d: tx_in(d).wait_recv(), TOP)
        ag[i] = (zx[0] + zx[1] + zx[2]).astype(BF16).astype(F32)

    each(lambda d: sg(ag, g_s, g_r, d).start())

    finish(0)
    multiply(shard(1, 0))
    pass_on(2)

    each(lambda d: sg_in(ag, g_s, g_r, d).wait_recv())
    low_b = ag[0:8].reshape(64, N * N).astype(BF16)
    gp = ADAPTER_SCALING * dot_nt(low_b, og[...])
    for t in range(N):
        gus[t] = gp[t * 4 : (t + 1) * 4, :]
    gur[g] = gus[g]
    each(lambda d: gx(gus, gur, u_s, u_r, d).start())
    bl = ag[8 + lax.div(i, 2)].astype(BF16)
    low_half = lax.rem(i, 2) == 0

    def down(t, carry):
        full = ADAPTER_SCALING * dot_nn(bl, xv[:, pl.ds(pl.multiple_of(t * cols, cols), cols)])
        gds[t] = jnp.where(low_half, full[0:4, :], full[4:8, :])
        return carry

    lax.fori_loop(0, N, down, 0)
    gdr[g] = gds[g]
    each(lambda d: gx(gds, gdr, d_s, d_r, d).start())

    x_send(3, start)

    finish(1)
    multiply(shard(2, 0))
    finish(2)
    multiply(shard(3, 0))

    each(lambda d: gx_in(gus, gur, u_s, u_r, d).wait_recv())
    total_up = gur[0]
    for j in range(1, N):
        total_up = total_up + gur[j]
    gup_ref[...] = total_up[:, 0:hidden]
    each(lambda d: gx_in(gds, gdr, d_s, d_r, d).wait_recv())
    total_down = gdr[0]
    for j in range(1, N):
        total_down = total_down + gdr[j]
    gda[i] = total_down
    each(lambda d: sg(gda, e_s, e_r, d).start())

    pass_on(3)
    acc[...] += ADAPTER_SCALING * dot_nn(upt[0:ROWS, :], low_b)
    finish(3)
    proj_ref[...] = acc[0:hidden, :].astype(BF16)

    each(lambda d: sg_in(gda, e_s, e_r, d).wait_recv())
    for j in range(M):
        gdown_ref[j * 4 : (j + 1) * 4, :] = gda[j]

    each(lambda d: gx(hs, hr, h_s, h_r, d).wait_send())

    @pl.when(x == a)
    def _():
        each(lambda d: ax(d).wait_send())

    z_first(done)
    for k in range(1, SIDE):
        z_next(k, done)
    for k in range(SIDE):
        x_send(k, done)
        x_pass(k, done)
    each(lambda d: sx(red, rs, r_s, r_r, d).wait_send())

    @pl.when(i >= 8)
    def _():
        each(lambda d: tx(d).wait_send(), TOP)

    each(lambda d: sg(ag, g_s, g_r, d).wait_send())
    each(lambda d: gx(gus, gur, u_s, u_r, d).wait_send())
    each(lambda d: gx(gds, gdr, d_s, d_r, d).wait_send())
    each(lambda d: sg(gda, e_s, e_r, d).wait_send())


def on_device(
    hidden_input_slots,
    base_weight,
    adapter_a,
    adapter_up_matrix,
    upstream,
    logp_new,
    logp_old,
    rewards,
    comp_lengths,
    assignment,
):
    tokens, depth = hidden_input_slots.shape
    share, hidden = base_weight.shape
    rank = adapter_a.shape[1]
    vmem = pl.BlockSpec(memory_space=pltpu.VMEM)
    dma = pltpu.SemaphoreType.DMA
    projection, down, up, loss = pl.pallas_call(
        kernel,
        out_shape=(
            jax.ShapeDtypeStruct((hidden, tokens), BF16),
            jax.ShapeDtypeStruct((rank, share), F32),
            jax.ShapeDtypeStruct((rank // N, hidden), F32),
            jax.ShapeDtypeStruct((1, 1), F32),
        ),
        in_specs=[pl.BlockSpec(memory_space=pl.ANY)] + [vmem] * 9,
        out_specs=(vmem,) * 4,
        scratch_shapes=[
            pltpu.VMEM((tokens, depth), BF16),
            pltpu.VMEM((N, ROWS, share), BF16),
            pltpu.VMEM((ROWS, tokens), F32),
            pltpu.VMEM((rank, 384), BF16),
            pltpu.VMEM((384, rank), BF16),
            pltpu.VMEM((384, tokens), BF16),
            pltpu.VMEM((8, tokens), F32),
            pltpu.VMEM((N, tokens), F32),
            pltpu.VMEM((N, 8, tokens), F32),
            pltpu.VMEM((N, 8, tokens), F32),
            pltpu.VMEM((SIDE, rank, 128), BF16),
            pltpu.VMEM((M, 8, tokens), F32),
            pltpu.VMEM((M, 8, tokens), F32),
            pltpu.VMEM((TOP, 8, tokens), F32),
            pltpu.VMEM((M, 8, tokens), F32),
            pltpu.VMEM((N, 4, 384), F32),
            pltpu.VMEM((N, 4, 384), F32),
            pltpu.VMEM((N, 4, share), F32),
            pltpu.VMEM((N, 4, share), F32),
            pltpu.VMEM((M, 4, share), F32),
            dma,
            dma((N,)), dma((N,)),
            dma((N,)), dma((SIDE,)),
            dma((5, 2)), dma((SIDE, 2, 2)), dma((SIDE, 2)), dma((N, 2)),
            dma((M,)), dma((M,)),
            dma((TOP,)), dma((TOP,)),
            dma((M,)), dma((M,)),
            dma((N,)), dma((N,)),
            dma((N,)), dma((N,)),
            dma((M,)), dma((M,)),
        ],
        compiler_params=pltpu.CompilerParams(collective_id=0, has_side_effects=True),
    )(
        hidden_input_slots,
        base_weight.T,
        adapter_a.T,
        adapter_up_matrix,
        upstream.T,
        logp_new,
        logp_old,
        rewards,
        comp_lengths,
        assignment,
    )
    return (projection.T, down.T, up, loss.reshape(1))


def solution(mesh):
    return jax.shard_map(
        on_device,
        mesh=mesh,
        in_specs=(
            P("group", None),
            P("group", "fsdp"),
            P("group", None),
            P(None, "fsdp"),
            P("group", "fsdp"),
            P("group", None, None),
            P("group", None, None),
            P("group", None),
            P("group", None),
            P("group", None),
        ),
        out_specs=(P("group", "fsdp"), P("group", None), P("group", "fsdp"), P("group")),
        check_vma=False,
    )
```

```python
import jax
import jax.numpy as jnp
from jax import lax
from jax.experimental import pallas as pl
from jax.experimental.pallas import tpu as pltpu
from jax.sharding import PartitionSpec as P

COMP = 16
ADAPTER_SCALING = 0.25
SPREAD_FLOOR = 0.16

N = 16
SIDE = 4
M = 16
TOP = 3
MESH = pl.DeviceIdType.MESH
ROWS = 320
SPLIT = 256
HALF = SPLIT // 2
REST = ROWS - SPLIT
F32 = jnp.float32
BF16 = jnp.bfloat16


def dot_nn(a, b):
    return lax.dot_general(a, b, (((1,), (0,)), ((), ())), preferred_element_type=F32)


def dot_nt(a, b):
    return lax.dot_general(a, b, (((1,), (1,)), ((), ())), preferred_element_type=F32)


def kernel(
    x_hbm, w_ref, a_ref, up_ref, ups_ref, new_ref, old_ref, rew_ref, len_ref, asg_ref,
    proj_ref, gdown_ref, gup_ref, loss_ref,
    xv, wg, acc, up_p, upt, og, row, tab, hs, hr, ag_a, red, rs, zx, ag, lows, gus, gur, gds, gdr, gda,
    x_sem, h_s, h_r, a_s, a_r, zs, xs, fs, w_r, qx_s, qx_r, qz_s, qz_r, r_s, r_r, z_s, z_r, g_s, g_r, u_s, u_r, d_s, d_r, e_s, e_r,
):
    g = lax.axis_index("group")
    f = lax.axis_index("fsdp")
    z, x = lax.div(g, SIDE), lax.rem(g, SIDE)
    zh, i = lax.div(f, M), lax.rem(f, M)
    a, b = lax.div(i, SIDE), lax.rem(i, SIDE)
    hidden = w_ref.shape[0]
    cols = w_ref.shape[1]

    def copy(src, dst, ss, rr, tg, tf):
        return pltpu.make_async_remote_copy(
            src_ref=src, dst_ref=dst, send_sem=ss, recv_sem=rr,
            device_id=(tg, tf), device_id_type=MESH,
        )

    def each(fn, count=N):
        def body(d, carry):
            fn(d)
            return carry

        lax.fori_loop(1, count, body, 0)

    def group_to(d):
        return lax.rem(g + d, N)

    def group_from(d):
        return lax.rem(g + N - d, N)

    def side_to(d):
        return lax.rem(i + d, M)

    def side_from(d):
        return lax.rem(i + M - d, M)

    def top_to(d):
        return lax.rem(zh + d, TOP)

    def top_from(d):
        return lax.rem(zh + TOP - d, TOP)

    def gx(src, dst, ss, rr, d):
        return copy(src.at[group_to(d)], dst.at[g], ss.at[d], rr.at[d], group_to(d), f)

    def gx_in(src, dst, ss, rr, d):
        j = group_from(d)
        return copy(src.at[j], dst.at[j], ss.at[d], rr.at[d], j, f)

    def sx(src, dst, ss, rr, d):
        return copy(src.at[side_to(d)], dst.at[i], ss.at[d], rr.at[d], g, zh * M + side_to(d))

    def sx_in(src, dst, ss, rr, d):
        j = side_from(d)
        return copy(src.at[j], dst.at[j], ss.at[d], rr.at[d], g, zh * M + j)

    def sg(buf, ss, rr, d):
        return copy(buf.at[i], buf.at[i], ss.at[d], rr.at[d], g, zh * M + side_to(d))

    def sg_in(buf, ss, rr, d):
        j = side_from(d)
        return copy(buf.at[j], buf.at[j], ss.at[d], rr.at[d], g, zh * M + j)

    def tx(d):
        return copy(zx.at[zh], zx.at[zh], z_s.at[d], z_r.at[d], g, top_to(d) * M + i)

    def tx_in(d):
        j = top_from(d)
        return copy(zx.at[j], zx.at[j], z_s.at[d], z_r.at[d], g, j * M + i)

    x_copy = pltpu.make_async_copy(x_hbm, xv, x_sem)
    x_copy.start()

    barrier = pltpu.get_barrier_semaphore()

    def greet(d):
        pl.semaphore_signal(barrier, inc=1, device_id=(group_to(d), f), device_id_type=MESH)
        pl.semaphore_signal(barrier, inc=1, device_id=(g, zh * M + side_to(d)), device_id_type=MESH)

    each(greet)
    each(
        lambda d: pl.semaphore_signal(
            barrier, inc=1, device_id=(g, top_to(d) * M + i), device_id_type=MESH
        ),
        TOP,
    )

    wg[g, ROWS - 16 : ROWS, :] = jnp.zeros((16, cols), BF16)
    wg[g, 0:hidden, :] = w_ref[...]

    rewards = rew_ref[...]
    mean = jnp.sum(rewards, axis=1, keepdims=True) / COMP
    var = jnp.sum(rewards * rewards, axis=1, keepdims=True) / COMP - mean * mean
    spread = jnp.sqrt(jnp.maximum(var, SPREAD_FLOOR))
    advantage = (rewards - mean) / spread
    dest = asg_ref[...] == lax.broadcasted_iota(jnp.int32, (N, N), 0)
    lengths = len_ref[...].astype(F32)
    old = old_ref[0]
    sent_old = jnp.zeros((N, N), F32)
    for k in range(N):
        sent_old = jnp.where(dest[:, k : k + 1], old[k : k + 1, :], sent_old)
    sent_adv = jnp.sum(jnp.where(dest, advantage, 0.0), axis=1, keepdims=True)
    sent_len = jnp.sum(jnp.where(dest, lengths, 0.0), axis=1, keepdims=True)
    hs[...] = jnp.zeros(hs.shape, F32)
    for at, value in enumerate((sent_old, sent_adv, sent_len)):
        tab[...] = jnp.zeros(tab.shape, F32)
        tab[:, 0:N] = jnp.broadcast_to(value, (N, N))
        rolled = pltpu.roll(tab[...], g * N, axis=1)
        for t in range(N):
            hs[t, at : at + 1, :] = rolled[t : t + 1, :]
    hr[g] = hs[g]
    for j in range(N):
        row[0:1, j * N : (j + 1) * N] = new_ref[0, j : j + 1, :]

    up_p[...] = jnp.zeros(up_p.shape, BF16)
    up_p[:, 0:hidden] = up_ref[...]
    upt[...] = up_p[...].astype(F32).T.astype(BF16)
    og[...] = jnp.zeros(og.shape, BF16)

    pl.semaphore_wait(barrier, 2 * (N - 1) + TOP - 1)

    each(lambda d: gx(hs, hr, h_s, h_r, d).start())

    quarter = pl.ds(pl.multiple_of(b * 128, 128), 128)

    def ax(d):
        return copy(
            a_ref.at[:, quarter], ag_a.at[z], a_s.at[d], a_r.at[z], group_to(d), f
        )

    @pl.when(x == a)
    def _():
        ag_a[z] = a_ref[:, quarter]
        each(lambda d: ax(d).start())

    right = z * SIDE + lax.rem(x + 1, SIDE)
    left = z * SIDE + lax.rem(x + SIDE - 1, SIDE)

    def part(s, h):
        return wg.at[s, pl.ds(h * HALF, HALF), :]

    def wx(s, h, sem, tg):
        return copy(part(s, h), part(s, h), sem, w_r.at[s, h], tg, f)

    def arrive(s, h):
        wx(s, h, fs.at[0, 0], g).wait_recv()

    near = [z, z + 1 - 2 * lax.rem(z, 2), 2 - lax.div(z, 2), 3 - 3 * lax.div(z, 2)]
    inner = (z == 1) | (z == 2)
    beyond = [None, 3 - z, 3 * (z - 1), 3 * (z - 1)]

    def z_first(go):
        for h in (0, 1):

            @pl.when(z < SIDE - 1)
            def _():
                go(wx(g, h, zs.at[0, h], g + SIDE))

            @pl.when(z > 0)
            def _():
                go(wx(g, h, zs.at[4, h], g - SIDE))

    def z_next(k, go):
        for h in (0, 1):
            go(wx(near[k] * SIDE + x, h, zs.at[k, h], beyond[k] * SIDE + x))

    def x_send(k, go):
        s = near[k] * SIDE + x
        go(wx(s, 0, xs.at[k, 0, 0], right))
        go(wx(s, 1, xs.at[k, 1, 1], left))
        go(wx(s, 1, xs.at[k, 0, 1], right))
        go(wx(s, 0, xs.at[k, 1, 0], left))

    def shard(k, off):
        return near[k] * SIDE + lax.rem(x + off, SIDE)

    def x_pass(k, go):
        go(wx(shard(k, 3), 0, fs.at[k, 0], right))
        go(wx(shard(k, 1), 1, fs.at[k, 1], left))

    def start(c):
        c.start()

    def done(c):
        c.wait_send()

    def pass_on(k):
        arrive(shard(k, 3), 0)
        arrive(shard(k, 1), 1)
        x_pass(k, start)

    def land(k):
        arrive(near[k] * SIDE + x, 0)
        arrive(near[k] * SIDE + x, 1)

    def q_copy(ref, sem, rem, tg):
        return copy(ref, ref, sem, rem, tg, f)

    def q_part(s):
        return wg.at[s, pl.ds(SPLIT, REST), :]

    def q_half(s, h):
        return wg.at[s, pl.ds(SPLIT + h * (REST // 2), REST // 2), :]

    def q_rows(zz):
        return wg.at[pl.ds(zz * SIDE, SIDE), pl.ds(SPLIT, REST), :]

    def q_send(go):
        go(q_copy(q_part(g), qx_s.at[0], qx_r.at[0], right))
        go(q_copy(q_part(g), qx_s.at[1], qx_r.at[1], left))

    def q_pass(go):
        go(q_copy(q_half(shard(0, 3), 0), qx_s.at[2], qx_r.at[2], right))
        go(q_copy(q_half(shard(0, 1), 1), qx_s.at[3], qx_r.at[3], left))

    def q_first(go):
        @pl.when(z < SIDE - 1)
        def _():
            go(q_copy(q_rows(z), qz_s.at[0], qz_r.at[z], g + SIDE))

        @pl.when(z > 0)
        def _():
            go(q_copy(q_rows(z), qz_s.at[4], qz_r.at[z], g - SIDE))

    def q_next(k, go):
        go(q_copy(q_rows(near[k]), qz_s.at[k], qz_r.at[near[k]], beyond[k] * SIDE + x))

    def q_land(k):
        q_copy(q_rows(near[k]), qz_s.at[0], qz_r.at[near[k]], g).wait_recv()

    def q_relay(k):
        @pl.when(inner)
        def _():
            q_land(k)
            q_next(k, start)

    def x_block(s):
        return xv[:, pl.ds(pl.multiple_of(s * cols, cols), cols)]

    def multiply(s, first=False):
        piece = dot_nt(wg[s, 0:SPLIT, :], x_block(s))
        if first:
            acc[0:SPLIT, :] = piece
        else:
            acc[0:SPLIT, :] += piece

    def q_multiply(k, first=False):
        piece = None
        for off in range(SIDE):
            s = near[k] * SIDE + off
            term = dot_nt(wg[s, SPLIT:ROWS, :], x_block(s))
            piece = term if piece is None else piece + term
        if first:
            acc[SPLIT:ROWS, :] = piece
        else:
            acc[SPLIT:ROWS, :] += piece

    def finish(k):
        arrive(shard(k, 3), 1)
        multiply(shard(k, 3))
        arrive(shard(k, 1), 0)
        multiply(shard(k, 1))
        arrive(shard(k, 2), 0)
        arrive(shard(k, 2), 1)
        multiply(shard(k, 2))

    q_send(start)
    z_first(start)
    x_send(0, start)

    each(lambda d: gx_in(hs, hr, h_s, h_r, d).wait_recv())
    got = hr[0]
    for j in range(1, N):
        got = got + hr[j]
    recv_old, recv_adv, recv_len = got[0:1, :], got[1:2, :], got[2:3, :]
    position = lax.rem(lax.broadcasted_iota(jnp.int32, (1, N * N), 1), N).astype(F32)
    ratio = jnp.exp(row[0:1, :] - recv_old)
    coef = jnp.where(position < recv_len, -(recv_adv * ratio) / (recv_len * COMP), 0.0)
    loss_ref[...] = jnp.sum(coef, axis=1, keepdims=True)
    og[0:hidden, :] = (coef * ups_ref[...].astype(F32)).astype(BF16)
    back = dot_nn(up_p[...], og[...])
    for p in range(M):
        red[p, 4:8, :] = back[p * 4 : (p + 1) * 4, :]

    q_copy(q_part(shard(0, 3)), qx_s.at[0], qx_r.at[0], g).wait_recv()
    q_copy(q_part(shard(0, 1)), qx_s.at[0], qx_r.at[1], g).wait_recv()
    q_pass(start)

    for q in range(SIDE):

        @pl.when((x != a) | (z != q))
        def _():
            copy(
                a_ref.at[:, quarter], ag_a.at[q], a_s.at[0], a_r.at[q], g, f
            ).wait_recv()

    x_copy.wait()
    low = jnp.zeros((64, N * N), F32)
    for q in range(SIDE):
        at = (q * SIDE + a) * cols + b * 128
        low = low + dot_nt(ag_a[q], xv[:, pl.ds(pl.multiple_of(at, 128), 128)])
    for p in range(M):
        red[p, 0:4, :] = low[p * 4 : (p + 1) * 4, :]
    rs[i] = red[i]
    each(lambda d: sx(red, rs, r_s, r_r, d).start())

    pass_on(0)
    land(1)

    @pl.when(inner)
    def _():
        z_next(1, start)

    x_send(1, start)

    @pl.when(inner)
    def _():
        land(2)
        z_next(2, start)

    q_copy(q_half(shard(0, 2), 0), qx_s.at[0], qx_r.at[2], g).wait_recv()
    q_copy(q_half(shard(0, 2), 1), qx_s.at[0], qx_r.at[3], g).wait_recv()
    q_first(start)
    multiply(g, first=True)

    each(lambda d: sx_in(red, rs, r_s, r_r, d).wait_recv())
    total = rs[0]
    for j in range(1, M):
        total = total + rs[j]
    zx[zh] = total
    each(lambda d: tx(d).start(), TOP)
    ag[i] = total[0:4, :].astype(BF16).astype(F32)
    each(lambda d: sg(ag, g_s, g_r, d).start())

    @pl.when(inner)
    def _():
        land(3)
        z_next(3, start)

    pass_on(1)
    q_relay(1)

    each(lambda d: tx_in(d).wait_recv(), TOP)
    bl = (zx[0] + zx[1] + zx[2]).astype(BF16)

    def down(t, carry):
        full = ADAPTER_SCALING * dot_nn(bl, x_block(t))
        gds[t] = full[4:8, :]
        return carry

    lax.fori_loop(0, N, down, 0)
    gdr[g] = gds[g]
    each(lambda d: gx(gds, gdr, d_s, d_r, d).start())

    @pl.when(jnp.logical_not(inner))
    def _():
        land(2)

    x_send(2, start)
    q_relay(2)
    finish(0)
    multiply(shard(1, 0))

    each(lambda d: sg_in(ag, g_s, g_r, d).wait_recv())
    for j in range(M):
        lows[j * 4 : (j + 1) * 4, :] = ag[j]
    low_b = lows[...].astype(BF16)
    gp = ADAPTER_SCALING * dot_nt(low_b, og[...])
    for t in range(N):
        gus[t] = gp[t * 4 : (t + 1) * 4, :]
    gur[g] = gus[g]
    each(lambda d: gx(gus, gur, u_s, u_r, d).start())

    pass_on(2)

    @pl.when(jnp.logical_not(inner))
    def _():
        land(3)

    x_send(3, start)
    q_relay(3)

    each(lambda d: gx_in(gds, gdr, d_s, d_r, d).wait_recv())
    total_down = gdr[0]
    for j in range(1, N):
        total_down = total_down + gdr[j]
    gda[i] = total_down
    each(lambda d: sg(gda, e_s, e_r, d).start())

    q_multiply(0, first=True)
    finish(1)
    multiply(shard(2, 0))
    acc[...] += ADAPTER_SCALING * dot_nn(upt[0:ROWS, :], low_b)
    each(lambda d: gx_in(gus, gur, u_s, u_r, d).wait_recv())
    total_up = gur[0]
    for j in range(1, N):
        total_up = total_up + gur[j]
    gup_ref[...] = total_up[:, 0:hidden]

    pass_on(3)
    multiply(shard(3, 0))
    each(lambda d: sg_in(gda, e_s, e_r, d).wait_recv())
    for j in range(M):
        gdown_ref[j * 4 : (j + 1) * 4, :] = gda[j]
    finish(2)
    for k in (1, 2):

        @pl.when(jnp.logical_not(inner))
        def _():
            q_land(k)

        q_multiply(k)

    finish(3)

    @pl.when(jnp.logical_not(inner))
    def _():
        q_land(3)

    q_multiply(3)
    proj_ref[...] = acc[0:hidden, :].astype(BF16)

    each(lambda d: gx(hs, hr, h_s, h_r, d).wait_send())

    @pl.when(x == a)
    def _():
        each(lambda d: ax(d).wait_send())

    q_send(done)
    q_pass(done)
    q_first(done)
    z_first(done)

    @pl.when(inner)
    def _():
        for k in range(1, SIDE):
            z_next(k, done)
            q_next(k, done)

    for k in range(SIDE):
        x_send(k, done)
        x_pass(k, done)
    each(lambda d: sx(red, rs, r_s, r_r, d).wait_send())
    each(lambda d: tx(d).wait_send(), TOP)
    each(lambda d: sg(ag, g_s, g_r, d).wait_send())
    each(lambda d: gx(gus, gur, u_s, u_r, d).wait_send())
    each(lambda d: gx(gds, gdr, d_s, d_r, d).wait_send())
    each(lambda d: sg(gda, e_s, e_r, d).wait_send())


def on_device(
    hidden_input_slots,
    base_weight,
    adapter_a,
    adapter_up_matrix,
    upstream,
    logp_new,
    logp_old,
    rewards,
    comp_lengths,
    assignment,
):
    tokens, depth = hidden_input_slots.shape
    share, hidden = base_weight.shape
    rank = adapter_a.shape[1]
    vmem = pl.BlockSpec(memory_space=pltpu.VMEM)
    dma = pltpu.SemaphoreType.DMA
    projection, down, up, loss = pl.pallas_call(
        kernel,
        out_shape=(
            jax.ShapeDtypeStruct((hidden, tokens), BF16),
            jax.ShapeDtypeStruct((rank, share), F32),
            jax.ShapeDtypeStruct((rank // N, hidden), F32),
            jax.ShapeDtypeStruct((1, 1), F32),
        ),
        in_specs=[pl.BlockSpec(memory_space=pl.ANY)] + [vmem] * 9,
        out_specs=(vmem,) * 4,
        scratch_shapes=[
            pltpu.VMEM((tokens, depth), BF16),
            pltpu.VMEM((N, ROWS, share), BF16),
            pltpu.VMEM((ROWS, tokens), F32),
            pltpu.VMEM((rank, 384), BF16),
            pltpu.VMEM((384, rank), BF16),
            pltpu.VMEM((384, tokens), BF16),
            pltpu.VMEM((8, tokens), F32),
            pltpu.VMEM((N, tokens), F32),
            pltpu.VMEM((N, 8, tokens), F32),
            pltpu.VMEM((N, 8, tokens), F32),
            pltpu.VMEM((SIDE, rank, 128), BF16),
            pltpu.VMEM((M, 8, tokens), F32),
            pltpu.VMEM((M, 8, tokens), F32),
            pltpu.VMEM((TOP, 8, tokens), F32),
            pltpu.VMEM((M, 4, tokens), F32),
            pltpu.VMEM((rank, tokens), F32),
            pltpu.VMEM((N, 4, 384), F32),
            pltpu.VMEM((N, 4, 384), F32),
            pltpu.VMEM((N, 4, share), F32),
            pltpu.VMEM((N, 4, share), F32),
            pltpu.VMEM((M, 4, share), F32),
            dma,
            dma((N,)), dma((N,)),
            dma((N,)), dma((SIDE,)),
            dma((5, 2)), dma((SIDE, 2, 2)), dma((SIDE, 2)), dma((N, 2)),
            dma((4,)), dma((4,)), dma((5,)), dma((SIDE,)),
            dma((M,)), dma((M,)),
            dma((TOP,)), dma((TOP,)),
            dma((M,)), dma((M,)),
            dma((N,)), dma((N,)),
            dma((N,)), dma((N,)),
            dma((M,)), dma((M,)),
        ],
        compiler_params=pltpu.CompilerParams(collective_id=0, has_side_effects=True),
    )(
        hidden_input_slots,
        base_weight.T,
        adapter_a.T,
        adapter_up_matrix,
        upstream.T,
        logp_new,
        logp_old,
        rewards,
        comp_lengths,
        assignment,
    )
    return (projection.T, down.T, up, loss.reshape(1))


def solution(mesh):
    return jax.shard_map(
        on_device,
        mesh=mesh,
        in_specs=(
            P("group", None),
            P("group", "fsdp"),
            P("group", None),
            P(None, "fsdp"),
            P("group", "fsdp"),
            P("group", None, None),
            P("group", None, None),
            P("group", None),
            P("group", None),
            P("group", None),
        ),
        out_specs=(P("group", "fsdp"), P("group", None), P("group", "fsdp"), P("group")),
        check_vma=False,
    )
```

```python
import jax
import jax.numpy as jnp
from jax import lax
from jax.experimental import pallas as pl
from jax.experimental.pallas import tpu as pltpu
from jax.sharding import PartitionSpec as P

COMP = 16
ADAPTER_SCALING = 0.25
SPREAD_FLOOR = 0.16

N = 16
SIDE = 4
M = 16
TOP = 3
MESH = pl.DeviceIdType.MESH
ROWS = 320
SPLIT = 256
HALF = SPLIT // 2
REST = ROWS - SPLIT
F32 = jnp.float32
BF16 = jnp.bfloat16


def dot_nn(a, b):
    return lax.dot_general(a, b, (((1,), (0,)), ((), ())), preferred_element_type=F32)


def dot_nt(a, b):
    return lax.dot_general(a, b, (((1,), (1,)), ((), ())), preferred_element_type=F32)


def kernel(
    x_hbm, w_ref, a_ref, up_ref, ups_ref, new_ref, old_ref, rew_ref, len_ref, asg_ref,
    proj_ref, gdown_ref, gup_ref, loss_ref,
    xv, wg, acc, up_p, upt, og, row, tab, hs, hr, ag_a, red, rs, zx, ag, lows, gus, gur, gds, gdr, gda,
    x_sem, h_s, h_r, a_s, a_r, zs, xs, fs, w_r, qx_s, qx_r, qz_s, qz_r, r_s, r_r, z_s, z_r, g_s, g_r, u_s, u_r, d_s, d_r, e_s, e_r,
):
    g = lax.axis_index("group")
    f = lax.axis_index("fsdp")
    z, x = lax.div(g, SIDE), lax.rem(g, SIDE)
    zh, i = lax.div(f, M), lax.rem(f, M)
    a, b = lax.div(i, SIDE), lax.rem(i, SIDE)
    hidden = w_ref.shape[0]
    cols = w_ref.shape[1]

    def copy(src, dst, ss, rr, tg, tf):
        return pltpu.make_async_remote_copy(
            src_ref=src, dst_ref=dst, send_sem=ss, recv_sem=rr,
            device_id=(tg, tf), device_id_type=MESH,
        )

    def each(fn, count=N):
        def body(d, carry):
            fn(d)
            return carry

        lax.fori_loop(1, count, body, 0)

    def group_to(d):
        return lax.rem(g + d, N)

    def group_from(d):
        return lax.rem(g + N - d, N)

    def side_to(d):
        return lax.rem(i + d, M)

    def side_from(d):
        return lax.rem(i + M - d, M)

    def top_to(d):
        return lax.rem(zh + d, TOP)

    def top_from(d):
        return lax.rem(zh + TOP - d, TOP)

    def gx(src, dst, ss, rr, d):
        return copy(src.at[group_to(d)], dst.at[g], ss.at[d], rr.at[d], group_to(d), f)

    def gx_in(src, dst, ss, rr, d):
        j = group_from(d)
        return copy(src.at[j], dst.at[j], ss.at[d], rr.at[d], j, f)

    def sx(src, dst, ss, rr, d):
        return copy(src.at[side_to(d)], dst.at[i], ss.at[d], rr.at[d], g, zh * M + side_to(d))

    def sx_in(src, dst, ss, rr, d):
        j = side_from(d)
        return copy(src.at[j], dst.at[j], ss.at[d], rr.at[d], g, zh * M + j)

    def sg(buf, ss, rr, d):
        return copy(buf.at[i], buf.at[i], ss.at[d], rr.at[d], g, zh * M + side_to(d))

    def sg_in(buf, ss, rr, d):
        j = side_from(d)
        return copy(buf.at[j], buf.at[j], ss.at[d], rr.at[d], g, zh * M + j)

    def tx(d):
        return copy(zx.at[zh], zx.at[zh], z_s.at[d], z_r.at[d], g, top_to(d) * M + i)

    def tx_in(d):
        j = top_from(d)
        return copy(zx.at[j], zx.at[j], z_s.at[d], z_r.at[d], g, j * M + i)

    x_copy = pltpu.make_async_copy(x_hbm, xv, x_sem)
    x_copy.start()

    barrier = pltpu.get_barrier_semaphore()

    def greet(d):
        pl.semaphore_signal(barrier, inc=1, device_id=(group_to(d), f), device_id_type=MESH)
        pl.semaphore_signal(barrier, inc=1, device_id=(g, zh * M + side_to(d)), device_id_type=MESH)

    each(greet)
    each(
        lambda d: pl.semaphore_signal(
            barrier, inc=1, device_id=(g, top_to(d) * M + i), device_id_type=MESH
        ),
        TOP,
    )

    wg[g, ROWS - 16 : ROWS, :] = jnp.zeros((16, cols), BF16)
    wg[g, 0:hidden, :] = w_ref[...]

    rewards = rew_ref[...]
    mean = jnp.sum(rewards, axis=1, keepdims=True) / COMP
    var = jnp.sum(rewards * rewards, axis=1, keepdims=True) / COMP - mean * mean
    spread = jnp.sqrt(jnp.maximum(var, SPREAD_FLOOR))
    advantage = (rewards - mean) / spread
    dest = asg_ref[...] == lax.broadcasted_iota(jnp.int32, (N, N), 0)
    lengths = len_ref[...].astype(F32)
    old = old_ref[0]
    sent_old = jnp.zeros((N, N), F32)
    for k in range(N):
        sent_old = jnp.where(dest[:, k : k + 1], old[k : k + 1, :], sent_old)
    sent_adv = jnp.sum(jnp.where(dest, advantage, 0.0), axis=1, keepdims=True)
    sent_len = jnp.sum(jnp.where(dest, lengths, 0.0), axis=1, keepdims=True)
    hs[...] = jnp.zeros(hs.shape, F32)
    for at, value in enumerate((sent_old, sent_adv, sent_len)):
        tab[...] = jnp.zeros(tab.shape, F32)
        tab[:, 0:N] = jnp.broadcast_to(value, (N, N))
        rolled = pltpu.roll(tab[...], g * N, axis=1)
        for t in range(N):
            hs[t, at : at + 1, :] = rolled[t : t + 1, :]
    hr[g] = hs[g]
    for j in range(N):
        row[0:1, j * N : (j + 1) * N] = new_ref[0, j : j + 1, :]

    up_p[...] = jnp.zeros(up_p.shape, BF16)
    up_p[:, 0:hidden] = up_ref[...]
    upt[...] = up_p[...].astype(F32).T.astype(BF16)
    og[...] = jnp.zeros(og.shape, BF16)

    pl.semaphore_wait(barrier, 2 * (N - 1) + TOP - 1)

    quarter = pl.ds(pl.multiple_of(b * 128, 128), 128)

    def ax(d):
        return copy(
            a_ref.at[:, quarter], ag_a.at[z], a_s.at[d], a_r.at[z], group_to(d), f
        )

    gives = (x == a) & (z - 1 + lax.div(SIDE - z, SIDE) == zh)
    @pl.when(x == a)
    def _():
        ag_a[z] = a_ref[:, quarter]

    @pl.when(gives)
    def _():
        each(lambda d: ax(d).start())

    each(lambda d: gx(hs, hr, h_s, h_r, d).start())

    right = z * SIDE + lax.rem(x + 1, SIDE)
    left = z * SIDE + lax.rem(x + SIDE - 1, SIDE)

    def part(s, h):
        return wg.at[s, pl.ds(h * HALF, HALF), :]

    def wx(s, h, sem, tg):
        return copy(part(s, h), part(s, h), sem, w_r.at[s, h], tg, f)

    def arrive(s, h):
        wx(s, h, fs.at[0, 0], g).wait_recv()

    near = [z, z + 1 - 2 * lax.rem(z, 2), 2 - lax.div(z, 2), 3 - 3 * lax.div(z, 2)]
    inner = (z == 1) | (z == 2)
    outer = (z == 0) | (z == 3)
    beyond = [None, 3 - z, 3 * (z - 1), 3 * (z - 1)]

    def z_first(go):
        for h in (0, 1):

            @pl.when(z < SIDE - 1)
            def _():
                go(wx(g, h, zs.at[0, h], g + SIDE))

            @pl.when(z > 0)
            def _():
                go(wx(g, h, zs.at[4, h], g - SIDE))

    def z_next(k, go):
        for h in (0, 1):
            go(wx(near[k] * SIDE + x, h, zs.at[k, h], beyond[k] * SIDE + x))

    def x_send(k, go):
        s = near[k] * SIDE + x
        go(wx(s, 0, xs.at[k, 0, 0], right))
        go(wx(s, 1, xs.at[k, 1, 1], left))
        go(wx(s, 1, xs.at[k, 0, 1], right))
        go(wx(s, 0, xs.at[k, 1, 0], left))

    def shard(k, off):
        return near[k] * SIDE + lax.rem(x + off, SIDE)

    def x_pass(k, go):
        go(wx(shard(k, 3), 0, fs.at[k, 0], right))
        go(wx(shard(k, 1), 1, fs.at[k, 1], left))

    def start(c):
        c.start()

    def done(c):
        c.wait_send()

    def pass_on(k):
        arrive(shard(k, 3), 0)
        arrive(shard(k, 1), 1)
        x_pass(k, start)

    def land(k):
        arrive(near[k] * SIDE + x, 0)
        arrive(near[k] * SIDE + x, 1)

    def q_copy(ref, sem, rem, tg):
        return copy(ref, ref, sem, rem, tg, f)

    def q_part(s):
        return wg.at[s, pl.ds(SPLIT, REST), :]

    def q_half(s, h):
        return wg.at[s, pl.ds(SPLIT + h * (REST // 2), REST // 2), :]

    def q_rows(zz):
        return wg.at[pl.ds(zz * SIDE, SIDE), pl.ds(SPLIT, REST), :]

    def q_send(go):
        go(q_copy(q_part(g), qx_s.at[0], qx_r.at[0], right))
        go(q_copy(q_part(g), qx_s.at[1], qx_r.at[1], left))

    def q_pass(go):
        go(q_copy(q_half(shard(0, 3), 0), qx_s.at[2], qx_r.at[2], right))
        go(q_copy(q_half(shard(0, 1), 1), qx_s.at[3], qx_r.at[3], left))

    def q_first(go):
        @pl.when(z < SIDE - 1)
        def _():
            go(q_copy(q_rows(z), qz_s.at[0], qz_r.at[z], g + SIDE))

        @pl.when(z > 0)
        def _():
            go(q_copy(q_rows(z), qz_s.at[4], qz_r.at[z], g - SIDE))

    def q_next(k, go):
        go(q_copy(q_rows(near[k]), qz_s.at[k], qz_r.at[near[k]], beyond[k] * SIDE + x))

    def q_land(k):
        q_copy(q_rows(near[k]), qz_s.at[0], qz_r.at[near[k]], g).wait_recv()

    def q_relay(k):
        @pl.when(inner)
        def _():
            q_land(k)
            q_next(k, start)

    def x_block(s):
        return xv[:, pl.ds(pl.multiple_of(s * cols, cols), cols)]

    def multiply(s, first=False):
        piece = dot_nt(wg[s, 0:SPLIT, :], x_block(s))
        if first:
            acc[0:SPLIT, :] = piece
        else:
            acc[0:SPLIT, :] += piece

    def q_multiply(k, first=False):
        piece = None
        for off in range(SIDE):
            s = near[k] * SIDE + off
            term = dot_nt(wg[s, SPLIT:ROWS, :], x_block(s))
            piece = term if piece is None else piece + term
        if first:
            acc[SPLIT:ROWS, :] = piece
        else:
            acc[SPLIT:ROWS, :] += piece

    def finish(k):
        arrive(shard(k, 3), 1)
        multiply(shard(k, 3))
        arrive(shard(k, 1), 0)
        multiply(shard(k, 1))
        arrive(shard(k, 2), 0)
        arrive(shard(k, 2), 1)
        multiply(shard(k, 2))

    q_send(start)
    z_first(start)
    x_send(0, start)

    each(lambda d: gx_in(hs, hr, h_s, h_r, d).wait_recv())
    got = hr[0]
    for j in range(1, N):
        got = got + hr[j]
    recv_old, recv_adv, recv_len = got[0:1, :], got[1:2, :], got[2:3, :]
    position = lax.rem(lax.broadcasted_iota(jnp.int32, (1, N * N), 1), N).astype(F32)
    ratio = jnp.exp(row[0:1, :] - recv_old)
    coef = jnp.where(position < recv_len, -(recv_adv * ratio) / (recv_len * COMP), 0.0)
    loss_ref[...] = jnp.sum(coef, axis=1, keepdims=True)
    og[0:hidden, :] = (coef * ups_ref[...].astype(F32)).astype(BF16)
    back = dot_nn(up_p[...], og[...])
    for p in range(M):
        red[p, 4:8, :] = back[p * 4 : (p + 1) * 4, :]

    q_copy(q_part(shard(0, 3)), qx_s.at[0], qx_r.at[0], g).wait_recv()
    q_copy(q_part(shard(0, 1)), qx_s.at[0], qx_r.at[1], g).wait_recv()
    q_pass(start)

    def adapter(q, at_first):
        @pl.when((x != a) | (z != q))
        def _():
            copy(
                a_ref.at[:, quarter], ag_a.at[q], a_s.at[0], a_r.at[q], g, f
            ).wait_recv()

        at = (q * SIDE + a) * cols + b * 128
        term = dot_nt(ag_a[q], xv[:, pl.ds(pl.multiple_of(at, 128), 128)])
        if at_first:
            lows[...] = term
        else:
            lows[...] += term

    x_copy.wait()
    adapter(zh + 1, True)

    @pl.when(zh == 0)
    def _():
        adapter(0, False)

    low = lows[...]
    for p in range(M):
        red[p, 0:4, :] = low[p * 4 : (p + 1) * 4, :]
    rs[i] = red[i]
    each(lambda d: sx(red, rs, r_s, r_r, d).start())

    pass_on(0)
    land(1)

    @pl.when(inner)
    def _():
        z_next(1, start)

    x_send(1, start)

    @pl.when(inner)
    def _():
        land(2)
        z_next(2, start)
        x_send(2, start)

    multiply(g, first=True)

    each(lambda d: sx_in(red, rs, r_s, r_r, d).wait_recv())
    total = rs[0]
    for j in range(1, M):
        total = total + rs[j]
    zx[zh] = total
    each(lambda d: tx(d).start(), TOP)

    q_copy(q_half(shard(0, 2), 0), qx_s.at[0], qx_r.at[2], g).wait_recv()
    q_copy(q_half(shard(0, 2), 1), qx_s.at[0], qx_r.at[3], g).wait_recv()

    @pl.when(inner)
    def _():
        land(3)
        z_next(3, start)

    q_first(start)

    @pl.when(outer)
    def _():
        land(2)
        x_send(2, start)

    pass_on(1)

    each(lambda d: tx_in(d).wait_recv(), TOP)
    whole = zx[0] + zx[1] + zx[2]
    ag[i] = whole[0:4, :].astype(BF16).astype(F32)
    each(lambda d: sg(ag, g_s, g_r, d).start())
    bl = whole.astype(BF16)

    def down(t, carry):
        for u in range(SIDE):
            full = ADAPTER_SCALING * dot_nn(bl, x_block(t * SIDE + u))
            gds[t * SIDE + u] = full[4:8, :]
        return carry

    lax.fori_loop(0, SIDE, down, 0)
    gdr[g] = gds[g]
    each(lambda d: gx(gds, gdr, d_s, d_r, d).start())

    pass_on(2)

    @pl.when(outer)
    def _():
        land(3)

    x_send(3, start)
    q_relay(1)
    q_relay(2)
    finish(0)
    multiply(shard(1, 0))

    each(lambda d: sg_in(ag, g_s, g_r, d).wait_recv())
    for j in range(M):
        lows[j * 4 : (j + 1) * 4, :] = ag[j]
    low_b = lows[...].astype(BF16)
    gp = ADAPTER_SCALING * dot_nt(low_b, og[...])
    for t in range(N):
        gus[t] = gp[t * 4 : (t + 1) * 4, :]
    gur[g] = gus[g]
    each(lambda d: gx(gus, gur, u_s, u_r, d).start())

    q_relay(3)
    pass_on(3)

    each(lambda d: gx_in(gds, gdr, d_s, d_r, d).wait_recv())
    total_down = gdr[0]
    for j in range(1, N):
        total_down = total_down + gdr[j]
    gda[i] = total_down
    each(lambda d: sg(gda, e_s, e_r, d).start())

    q_multiply(0, first=True)
    acc[...] += ADAPTER_SCALING * dot_nn(upt[0:ROWS, :], low_b)
    finish(1)
    multiply(shard(2, 0))
    finish(2)
    multiply(shard(3, 0))
    for k in (1, 2):

        @pl.when(outer)
        def _():
            q_land(k)

        q_multiply(k)

    each(lambda d: gx_in(gus, gur, u_s, u_r, d).wait_recv())
    total_up = gur[0]
    for j in range(1, N):
        total_up = total_up + gur[j]
    gup_ref[...] = total_up[:, 0:hidden]

    @pl.when(outer)
    def _():
        q_land(3)

    q_multiply(3)
    each(lambda d: sg_in(gda, e_s, e_r, d).wait_recv())
    for j in range(M):
        gdown_ref[j * 4 : (j + 1) * 4, :] = gda[j]
    finish(3)
    proj_ref[...] = acc[0:hidden, :].astype(BF16)

    each(lambda d: gx(hs, hr, h_s, h_r, d).wait_send())

    @pl.when(gives)
    def _():
        each(lambda d: ax(d).wait_send())

    q_send(done)
    q_pass(done)
    q_first(done)
    z_first(done)

    @pl.when(inner)
    def _():
        for k in range(1, SIDE):
            z_next(k, done)
            q_next(k, done)

    for k in range(SIDE):
        x_send(k, done)
        x_pass(k, done)
    each(lambda d: sx(red, rs, r_s, r_r, d).wait_send())
    each(lambda d: tx(d).wait_send(), TOP)
    each(lambda d: sg(ag, g_s, g_r, d).wait_send())
    each(lambda d: gx(gus, gur, u_s, u_r, d).wait_send())
    each(lambda d: gx(gds, gdr, d_s, d_r, d).wait_send())
    each(lambda d: sg(gda, e_s, e_r, d).wait_send())


def keep(*refs):
    for taken, given in zip(refs[:4], refs[4:]):
        given[...] = taken[...]


def on_device(
    hidden_input_slots,
    base_weight,
    adapter_a,
    adapter_up_matrix,
    upstream,
    logp_new,
    logp_old,
    rewards,
    comp_lengths,
    assignment,
):
    tokens, depth = hidden_input_slots.shape
    share, hidden = base_weight.shape
    rank = adapter_a.shape[1]
    vmem = pl.BlockSpec(memory_space=pltpu.VMEM)
    dma = pltpu.SemaphoreType.DMA
    projection, down, up, loss = pl.pallas_call(
        kernel,
        out_shape=(
            jax.ShapeDtypeStruct((hidden, tokens), BF16),
            jax.ShapeDtypeStruct((rank, share), F32),
            jax.ShapeDtypeStruct((rank // N, hidden), F32),
            jax.ShapeDtypeStruct((1, 1), F32),
        ),
        in_specs=[pl.BlockSpec(memory_space=pl.ANY)] + [vmem] * 9,
        out_specs=(vmem,) * 4,
        scratch_shapes=[
            pltpu.VMEM((tokens, depth), BF16),
            pltpu.VMEM((N, ROWS, share), BF16),
            pltpu.VMEM((ROWS, tokens), F32),
            pltpu.VMEM((rank, 384), BF16),
            pltpu.VMEM((384, rank), BF16),
            pltpu.VMEM((384, tokens), BF16),
            pltpu.VMEM((8, tokens), F32),
            pltpu.VMEM((N, tokens), F32),
            pltpu.VMEM((N, 8, tokens), F32),
            pltpu.VMEM((N, 8, tokens), F32),
            pltpu.VMEM((SIDE, rank, 128), BF16),
            pltpu.VMEM((M, 8, tokens), F32),
            pltpu.VMEM((M, 8, tokens), F32),
            pltpu.VMEM((TOP, 8, tokens), F32),
            pltpu.VMEM((M, 4, tokens), F32),
            pltpu.VMEM((rank, tokens), F32),
            pltpu.VMEM((N, 4, 384), F32),
            pltpu.VMEM((N, 4, 384), F32),
            pltpu.VMEM((N, 4, share), F32),
            pltpu.VMEM((N, 4, share), F32),
            pltpu.VMEM((M, 4, share), F32),
            dma,
            dma((N,)), dma((N,)),
            dma((N,)), dma((SIDE,)),
            dma((5, 2)), dma((SIDE, 2, 2)), dma((SIDE, 2)), dma((N, 2)),
            dma((4,)), dma((4,)), dma((5,)), dma((SIDE,)),
            dma((M,)), dma((M,)),
            dma((TOP,)), dma((TOP,)),
            dma((M,)), dma((M,)),
            dma((N,)), dma((N,)),
            dma((N,)), dma((N,)),
            dma((M,)), dma((M,)),
        ],
        compiler_params=pltpu.CompilerParams(collective_id=0, has_side_effects=True),
    )(
        hidden_input_slots,
        base_weight.T,
        adapter_a.T,
        adapter_up_matrix,
        upstream.T,
        logp_new,
        logp_old,
        rewards,
        comp_lengths,
        assignment,
    )
    kept = pl.pallas_call(
        keep,
        out_shape=tuple(
            jax.ShapeDtypeStruct(v.shape, v.dtype) for v in (projection, down, up, loss)
        ),
        in_specs=[vmem] * 4,
        out_specs=(vmem,) * 4,
    )(projection, down, up, loss)
    projection, down, up, loss = kept
    return (projection.T, down.T, up, loss.reshape(1))


def solution(mesh):
    return jax.shard_map(
        on_device,
        mesh=mesh,
        in_specs=(
            P("group", None),
            P("group", "fsdp"),
            P("group", None),
            P(None, "fsdp"),
            P("group", "fsdp"),
            P("group", None, None),
            P("group", None, None),
            P("group", None),
            P("group", None),
            P("group", None),
        ),
        out_specs=(P("group", "fsdp"), P("group", None), P("group", "fsdp"), P("group")),
        check_vma=False,
    )
```

```python
import jax
import jax.numpy as jnp
from jax import lax
from jax.experimental import pallas as pl
from jax.experimental.pallas import tpu as pltpu
from jax.sharding import PartitionSpec as P

COMP = 16
ADAPTER_SCALING = 0.25
SPREAD_FLOOR = 0.16

N = 16
SIDE = 4
M = 16
TOP = 3
MESH = pl.DeviceIdType.MESH
ROWS = 308
SPLIT = 240
CUTS = ((0, 128), (128, 112))
REST = ROWS - SPLIT
Q_CUTS = ((SPLIT, 32), (SPLIT + 32, REST - 32))
F32 = jnp.float32
BF16 = jnp.bfloat16


def dot_nn(a, b):
    return lax.dot_general(a, b, (((1,), (0,)), ((), ())), preferred_element_type=F32)


def dot_nt(a, b):
    return lax.dot_general(a, b, (((1,), (1,)), ((), ())), preferred_element_type=F32)


def kernel(
    x_hbm, w_hbm, a_hbm, up_hbm, ups_hbm, new_hbm, old_hbm, rew_hbm, len_hbm, asg_hbm,
    proj_hbm, gdown_hbm, gup_hbm, loss_hbm,
    a_ref, up_ref, ups_ref, new_ref, old_ref, rew_ref, len_ref, asg_ref,
    proj_ref, gdown_ref, gup_ref, loss_ref, in_sem, out_sem,
    xv, wg, acc, up_p, upt, og, row, tab, hs, hr, ag_a, red, rs, zx, ag, lows, gus, gur, gds, gdr, gda,
    x_sem, h_s, h_r, a_s, a_r, zs, xs, fs, w_r, qx_s, qx_r, qz_s, qz_r, r_s, r_r, z_s, z_r, g_s, g_r, u_s, u_r, d_s, d_r, e_s, e_r,
):
    g = lax.axis_index("group")
    f = lax.axis_index("fsdp")
    z, x = lax.div(g, SIDE), lax.rem(g, SIDE)
    zh, i = lax.div(f, M), lax.rem(f, M)
    a, b = lax.div(i, SIDE), lax.rem(i, SIDE)
    hidden, cols = w_hbm.shape

    def copy(src, dst, ss, rr, tg, tf):
        return pltpu.make_async_remote_copy(
            src_ref=src, dst_ref=dst, send_sem=ss, recv_sem=rr,
            device_id=(tg, tf), device_id_type=MESH,
        )

    def each(fn, count=N):
        def body(d, carry):
            fn(d)
            return carry

        lax.fori_loop(1, count, body, 0)

    def group_to(d):
        return lax.rem(g + d, N)

    def group_from(d):
        return lax.rem(g + N - d, N)

    def side_to(d):
        return lax.rem(i + d, M)

    def side_from(d):
        return lax.rem(i + M - d, M)

    def top_to(d):
        return lax.rem(zh + d, TOP)

    def top_from(d):
        return lax.rem(zh + TOP - d, TOP)

    def gx(src, dst, ss, rr, d):
        return copy(src.at[group_to(d)], dst.at[g], ss.at[d], rr.at[d], group_to(d), f)

    def gx_in(src, dst, ss, rr, d):
        j = group_from(d)
        return copy(src.at[j], dst.at[j], ss.at[d], rr.at[d], j, f)

    def sx(src, dst, ss, rr, d):
        return copy(src.at[side_to(d)], dst.at[i], ss.at[d], rr.at[d], g, zh * M + side_to(d))

    def sx_in(src, dst, ss, rr, d):
        j = side_from(d)
        return copy(src.at[j], dst.at[j], ss.at[d], rr.at[d], g, zh * M + j)

    def sg(buf, ss, rr, d):
        return copy(buf.at[i], buf.at[i], ss.at[d], rr.at[d], g, zh * M + side_to(d))

    def sg_in(buf, ss, rr, d):
        j = side_from(d)
        return copy(buf.at[j], buf.at[j], ss.at[d], rr.at[d], g, zh * M + j)

    def tx(d):
        return copy(zx.at[zh], zx.at[zh], z_s.at[d], z_r.at[d], g, top_to(d) * M + i)

    def tx_in(d):
        j = top_from(d)
        return copy(zx.at[j], zx.at[j], z_s.at[d], z_r.at[d], g, j * M + i)

    barrier = pltpu.get_barrier_semaphore()

    def greet(d):
        pl.semaphore_signal(barrier, inc=1, device_id=(group_to(d), f), device_id_type=MESH)
        pl.semaphore_signal(barrier, inc=1, device_id=(g, zh * M + side_to(d)), device_id_type=MESH)

    each(greet)
    each(
        lambda d: pl.semaphore_signal(
            barrier, inc=1, device_id=(g, top_to(d) * M + i), device_id_type=MESH
        ),
        TOP,
    )

    small = [
        pltpu.make_async_copy(source, target, in_sem.at[at])
        for at, (source, target) in enumerate(
            (
                (rew_hbm, rew_ref), (asg_hbm, asg_ref), (len_hbm, len_ref), (old_hbm, old_ref),
                (new_hbm, new_ref), (up_hbm, up_ref), (a_hbm, a_ref), (ups_hbm, ups_ref),
                (w_hbm, wg.at[g]),
            )
        )
    ]
    for c in small:
        c.start()
    x_copy = pltpu.make_async_copy(x_hbm, xv, x_sem)
    x_copy.start()
    outs = [
        pltpu.make_async_copy(source, target, out_sem.at[at])
        for at, (source, target) in enumerate(
            (
                (loss_ref, loss_hbm), (gup_ref, gup_hbm),
                (gdown_ref, gdown_hbm), (proj_ref, proj_hbm),
            )
        )
    ]
    hs[...] = jnp.zeros(hs.shape, F32)
    up_p[...] = jnp.zeros(up_p.shape, BF16)
    og[...] = jnp.zeros(og.shape, BF16)
    for c in small:
        c.wait()

    rewards = rew_ref[...]
    mean = jnp.sum(rewards, axis=1, keepdims=True) / COMP
    var = jnp.sum(rewards * rewards, axis=1, keepdims=True) / COMP - mean * mean
    spread = jnp.sqrt(jnp.maximum(var, SPREAD_FLOOR))
    advantage = (rewards - mean) / spread
    dest = asg_ref[...] == lax.broadcasted_iota(jnp.int32, (N, N), 0)
    lengths = len_ref[...].astype(F32)
    old = old_ref[0]
    sent_old = jnp.zeros((N, N), F32)
    for k in range(N):
        sent_old = jnp.where(dest[:, k : k + 1], old[k : k + 1, :], sent_old)
    sent_adv = jnp.sum(jnp.where(dest, advantage, 0.0), axis=1, keepdims=True)
    sent_len = jnp.sum(jnp.where(dest, lengths, 0.0), axis=1, keepdims=True)
    for at, value in enumerate((sent_old, sent_adv, sent_len)):
        tab[...] = jnp.zeros(tab.shape, F32)
        tab[:, 0:N] = jnp.broadcast_to(value, (N, N))
        rolled = pltpu.roll(tab[...], g * N, axis=1)
        for t in range(N):
            hs[t, at : at + 1, :] = rolled[t : t + 1, :]
    hr[g] = hs[g]
    for j in range(N):
        row[0:1, j * N : (j + 1) * N] = new_ref[0, j : j + 1, :]

    up_p[:, 0:hidden] = up_ref[...]
    upt[...] = up_p[...].astype(F32).T.astype(BF16)

    pl.semaphore_wait(barrier, 2 * (N - 1) + TOP - 1)

    quarter = pl.ds(pl.multiple_of(b * 128, 128), 128)

    def ax(d):
        return copy(
            a_ref.at[:, quarter], ag_a.at[z], a_s.at[d], a_r.at[z], group_to(d), f
        )

    gives = (x == a) & (z - 1 + lax.div(SIDE - z, SIDE) == zh)
    @pl.when(x == a)
    def _():
        ag_a[z] = a_ref[:, quarter]

    @pl.when(gives)
    def _():
        each(lambda d: ax(d).start())

    each(lambda d: gx(hs, hr, h_s, h_r, d).start())

    right = z * SIDE + lax.rem(x + 1, SIDE)
    left = z * SIDE + lax.rem(x + SIDE - 1, SIDE)

    def part(s, h):
        return wg.at[s, pl.ds(*CUTS[h]), :]

    def wx(s, h, sem, tg):
        return copy(part(s, h), part(s, h), sem, w_r.at[s, h], tg, f)

    def arrive(s, h):
        wx(s, h, fs.at[0, 0], g).wait_recv()

    near = [z, z + 1 - 2 * lax.rem(z, 2), 2 - lax.div(z, 2), 3 - 3 * lax.div(z, 2)]
    inner = (z == 1) | (z == 2)
    outer = (z == 0) | (z == 3)
    beyond = [None, 3 - z, 3 * (z - 1), 3 * (z - 1)]

    def z_first(go):
        for h in (0, 1):

            @pl.when(z < SIDE - 1)
            def _():
                go(wx(g, h, zs.at[0, h], g + SIDE))

            @pl.when(z > 0)
            def _():
                go(wx(g, h, zs.at[4, h], g - SIDE))

    def z_next(k, go):
        for h in (0, 1):
            go(wx(near[k] * SIDE + x, h, zs.at[k, h], beyond[k] * SIDE + x))

    def x_send(k, go):
        s = near[k] * SIDE + x
        go(wx(s, 0, xs.at[k, 0, 0], right))
        go(wx(s, 1, xs.at[k, 1, 1], left))
        go(wx(s, 1, xs.at[k, 0, 1], right))
        go(wx(s, 0, xs.at[k, 1, 0], left))

    def shard(k, off):
        return near[k] * SIDE + lax.rem(x + off, SIDE)

    def x_pass(k, go):
        go(wx(shard(k, 3), 0, fs.at[k, 0], right))
        go(wx(shard(k, 1), 1, fs.at[k, 1], left))

    def start(c):
        c.start()

    def done(c):
        c.wait_send()

    def pass_on(k):
        arrive(shard(k, 3), 0)
        arrive(shard(k, 1), 1)
        x_pass(k, start)

    def land(k):
        arrive(near[k] * SIDE + x, 0)
        arrive(near[k] * SIDE + x, 1)

    def q_copy(ref, sem, rem, tg):
        return copy(ref, ref, sem, rem, tg, f)

    def q_part(s):
        return wg.at[s, pl.ds(SPLIT, REST), :]

    def q_half(s, h):
        return wg.at[s, pl.ds(*Q_CUTS[h]), :]

    def q_rows(zz):
        return wg.at[pl.ds(zz * SIDE, SIDE), pl.ds(SPLIT, REST), :]

    def q_send(go):
        go(q_copy(q_part(g), qx_s.at[0], qx_r.at[0], right))
        go(q_copy(q_part(g), qx_s.at[1], qx_r.at[1], left))

    def q_pass(go):
        go(q_copy(q_half(shard(0, 3), 0), qx_s.at[2], qx_r.at[2], right))
        go(q_copy(q_half(shard(0, 1), 1), qx_s.at[3], qx_r.at[3], left))

    def q_first(go):
        @pl.when(z < SIDE - 1)
        def _():
            go(q_copy(q_rows(z), qz_s.at[0], qz_r.at[z], g + SIDE))

        @pl.when(z > 0)
        def _():
            go(q_copy(q_rows(z), qz_s.at[4], qz_r.at[z], g - SIDE))

    def q_next(k, go):
        go(q_copy(q_rows(near[k]), qz_s.at[k], qz_r.at[near[k]], beyond[k] * SIDE + x))

    def q_land(k):
        q_copy(q_rows(near[k]), qz_s.at[0], qz_r.at[near[k]], g).wait_recv()

    def q_relay(k):
        @pl.when(inner)
        def _():
            q_land(k)
            q_next(k, start)

    def x_block(s):
        return xv[:, pl.ds(pl.multiple_of(s * cols, cols), cols)]

    def multiply(s, first=False):
        piece = dot_nt(wg[s, 0:SPLIT, :], x_block(s))
        if first:
            acc[0:SPLIT, :] = piece
        else:
            acc[0:SPLIT, :] += piece

    def q_multiply(k, first=False):
        piece = None
        for off in range(SIDE):
            s = near[k] * SIDE + off
            term = dot_nt(wg[s, SPLIT:ROWS, :], x_block(s))
            piece = term if piece is None else piece + term
        if first:
            acc[SPLIT:ROWS, :] = piece
        else:
            acc[SPLIT:ROWS, :] += piece

    def finish(k):
        arrive(shard(k, 3), 1)
        multiply(shard(k, 3))
        arrive(shard(k, 1), 0)
        multiply(shard(k, 1))
        arrive(shard(k, 2), 0)
        arrive(shard(k, 2), 1)
        multiply(shard(k, 2))

    q_send(start)
    z_first(start)
    x_send(0, start)

    each(lambda d: gx_in(hs, hr, h_s, h_r, d).wait_recv())
    got = hr[0]
    for j in range(1, N):
        got = got + hr[j]
    recv_old, recv_adv, recv_len = got[0:1, :], got[1:2, :], got[2:3, :]
    position = lax.rem(lax.broadcasted_iota(jnp.int32, (1, N * N), 1), N).astype(F32)
    ratio = jnp.exp(row[0:1, :] - recv_old)
    coef = jnp.where(position < recv_len, -(recv_adv * ratio) / (recv_len * COMP), 0.0)
    loss_ref[...] = jnp.sum(coef, axis=1, keepdims=True)
    outs[0].start()
    og[0:hidden, :] = (coef * ups_ref[...].astype(F32)).astype(BF16)
    back = dot_nn(up_p[...], og[...])
    for p in range(M):
        red[p, 4:8, :] = back[p * 4 : (p + 1) * 4, :]

    q_copy(q_part(shard(0, 3)), qx_s.at[0], qx_r.at[0], g).wait_recv()
    q_copy(q_part(shard(0, 1)), qx_s.at[0], qx_r.at[1], g).wait_recv()
    q_pass(start)

    def adapter(q, at_first):
        @pl.when((x != a) | (z != q))
        def _():
            copy(
                a_ref.at[:, quarter], ag_a.at[q], a_s.at[0], a_r.at[q], g, f
            ).wait_recv()

        at = (q * SIDE + a) * cols + b * 128
        term = dot_nt(ag_a[q], xv[:, pl.ds(pl.multiple_of(at, 128), 128)])
        if at_first:
            lows[...] = term
        else:
            lows[...] += term

    x_copy.wait()
    adapter(zh + 1, True)

    @pl.when(zh == 0)
    def _():
        adapter(0, False)

    low = lows[...]
    for p in range(M):
        red[p, 0:4, :] = low[p * 4 : (p + 1) * 4, :]
    rs[i] = red[i]
    each(lambda d: sx(red, rs, r_s, r_r, d).start())

    pass_on(0)
    land(1)

    @pl.when(inner)
    def _():
        z_next(1, start)

    x_send(1, start)

    @pl.when(inner)
    def _():
        land(2)
        z_next(2, start)
        x_send(2, start)

    multiply(g, first=True)

    each(lambda d: sx_in(red, rs, r_s, r_r, d).wait_recv())
    total = rs[0]
    for j in range(1, M):
        total = total + rs[j]
    zx[zh] = total
    each(lambda d: tx(d).start(), TOP)

    q_copy(q_half(shard(0, 2), 0), qx_s.at[0], qx_r.at[2], g).wait_recv()
    q_copy(q_half(shard(0, 2), 1), qx_s.at[0], qx_r.at[3], g).wait_recv()

    @pl.when(inner)
    def _():
        land(3)
        z_next(3, start)

    q_first(start)

    @pl.when(outer)
    def _():
        land(2)
        x_send(2, start)

    pass_on(1)

    each(lambda d: tx_in(d).wait_recv(), TOP)
    whole = zx[0] + zx[1] + zx[2]
    ag[i] = whole[0:4, :].astype(BF16).astype(F32)
    each(lambda d: sg(ag, g_s, g_r, d).start())
    bl = whole.astype(BF16)

    def down(t, carry):
        for u in range(SIDE):
            full = ADAPTER_SCALING * dot_nn(bl, x_block(t * SIDE + u))
            gds[t * SIDE + u] = full[4:8, :]
        return carry

    lax.fori_loop(0, SIDE, down, 0)
    gdr[g] = gds[g]
    each(lambda d: gx(gds, gdr, d_s, d_r, d).start())

    pass_on(2)

    @pl.when(outer)
    def _():
        land(3)

    x_send(3, start)
    q_relay(1)
    q_relay(2)
    finish(0)
    multiply(shard(1, 0))

    each(lambda d: sg_in(ag, g_s, g_r, d).wait_recv())
    for j in range(M):
        lows[j * 4 : (j + 1) * 4, :] = ag[j]
    low_b = lows[...].astype(BF16)
    gp = ADAPTER_SCALING * dot_nt(low_b, og[...])
    for t in range(N):
        gus[t] = gp[t * 4 : (t + 1) * 4, :]
    gur[g] = gus[g]
    each(lambda d: gx(gus, gur, u_s, u_r, d).start())

    q_relay(3)
    pass_on(3)

    each(lambda d: gx_in(gds, gdr, d_s, d_r, d).wait_recv())
    total_down = gdr[0]
    for j in range(1, N):
        total_down = total_down + gdr[j]
    gda[i] = total_down
    each(lambda d: sg(gda, e_s, e_r, d).start())

    q_multiply(0, first=True)
    acc[...] += ADAPTER_SCALING * dot_nn(upt[0:ROWS, :], low_b)
    finish(1)
    multiply(shard(2, 0))
    finish(2)
    multiply(shard(3, 0))
    for k in (1, 2):

        @pl.when(outer)
        def _():
            q_land(k)

        q_multiply(k)

    each(lambda d: gx_in(gus, gur, u_s, u_r, d).wait_recv())
    total_up = gur[0]
    for j in range(1, N):
        total_up = total_up + gur[j]
    gup_ref[...] = total_up[:, 0:hidden]
    outs[1].start()

    @pl.when(outer)
    def _():
        q_land(3)

    q_multiply(3)
    each(lambda d: sg_in(gda, e_s, e_r, d).wait_recv())
    for j in range(M):
        gdown_ref[j * 4 : (j + 1) * 4, :] = gda[j]
    outs[2].start()
    finish(3)
    proj_ref[...] = acc[...].astype(BF16)
    outs[3].start()

    each(lambda d: gx(hs, hr, h_s, h_r, d).wait_send())

    @pl.when(gives)
    def _():
        each(lambda d: ax(d).wait_send())

    q_send(done)
    q_pass(done)
    q_first(done)
    z_first(done)

    @pl.when(inner)
    def _():
        for k in range(1, SIDE):
            z_next(k, done)
            q_next(k, done)

    for k in range(SIDE):
        x_send(k, done)
        x_pass(k, done)
    each(lambda d: sx(red, rs, r_s, r_r, d).wait_send())
    each(lambda d: tx(d).wait_send(), TOP)
    each(lambda d: sg(ag, g_s, g_r, d).wait_send())
    each(lambda d: gx(gus, gur, u_s, u_r, d).wait_send())
    each(lambda d: gx(gds, gdr, d_s, d_r, d).wait_send())
    each(lambda d: sg(gda, e_s, e_r, d).wait_send())
    for c in outs:
        c.wait()


def keep(*refs):
    given, taken, held, come, go = refs[:4], refs[4:8], refs[8:12], refs[12], refs[13]
    loads = [pltpu.make_async_copy(given[n], held[n], come.at[n]) for n in range(4)]
    stores = [pltpu.make_async_copy(held[n], taken[n], go.at[n]) for n in range(4)]
    for c in loads:
        c.start()
    for load, store in zip(loads, stores):
        load.wait()
        store.start()
    for c in stores:
        c.wait()


def on_device(
    hidden_input_slots,
    base_weight,
    adapter_a,
    adapter_up_matrix,
    upstream,
    logp_new,
    logp_old,
    rewards,
    comp_lengths,
    assignment,
):
    tokens, depth = hidden_input_slots.shape
    share, hidden = base_weight.shape
    rank = adapter_a.shape[1]
    hbm = pl.BlockSpec(memory_space=pl.ANY)
    dma = pltpu.SemaphoreType.DMA
    projection, down, up, loss = pl.pallas_call(
        kernel,
        out_shape=(
            jax.ShapeDtypeStruct((hidden, tokens), BF16),
            jax.ShapeDtypeStruct((rank, share), F32),
            jax.ShapeDtypeStruct((rank // N, hidden), F32),
            jax.ShapeDtypeStruct((1, 1), F32),
        ),
        in_specs=[hbm] * 10,
        out_specs=(hbm,) * 4,
        scratch_shapes=[
            pltpu.VMEM((rank, share), BF16),
            pltpu.VMEM((rank, hidden), BF16),
            pltpu.VMEM((hidden, tokens), BF16),
            pltpu.VMEM(logp_new.shape, F32),
            pltpu.VMEM(logp_old.shape, F32),
            pltpu.VMEM(rewards.shape, F32),
            pltpu.VMEM(comp_lengths.shape, jnp.int32),
            pltpu.VMEM(assignment.shape, jnp.int32),
            pltpu.VMEM((hidden, tokens), BF16),
            pltpu.VMEM((rank, share), F32),
            pltpu.VMEM((rank // N, hidden), F32),
            pltpu.VMEM((1, 1), F32),
            dma((9,)),
            dma((4,)),
            pltpu.VMEM((tokens, depth), BF16),
            pltpu.VMEM((N, ROWS, share), BF16),
            pltpu.VMEM((ROWS, tokens), F32),
            pltpu.VMEM((rank, 384), BF16),
            pltpu.VMEM((384, rank), BF16),
            pltpu.VMEM((384, tokens), BF16),
            pltpu.VMEM((8, tokens), F32),
            pltpu.VMEM((N, tokens), F32),
            pltpu.VMEM((N, 4, tokens), F32),
            pltpu.VMEM((N, 4, tokens), F32),
            pltpu.VMEM((SIDE, rank, 128), BF16),
            pltpu.VMEM((M, 8, tokens), F32),
            pltpu.VMEM((M, 8, tokens), F32),
            pltpu.VMEM((TOP, 8, tokens), F32),
            pltpu.VMEM((M, 4, tokens), F32),
            pltpu.VMEM((rank, tokens), F32),
            pltpu.VMEM((N, 4, 384), F32),
            pltpu.VMEM((N, 4, 384), F32),
            pltpu.VMEM((N, 4, share), F32),
            pltpu.VMEM((N, 4, share), F32),
            pltpu.VMEM((M, 4, share), F32),
            dma,
            dma((N,)), dma((N,)),
            dma((N,)), dma((SIDE,)),
            dma((5, 2)), dma((SIDE, 2, 2)), dma((SIDE, 2)), dma((N, 2)),
            dma((4,)), dma((4,)), dma((5,)), dma((SIDE,)),
            dma((M,)), dma((M,)),
            dma((TOP,)), dma((TOP,)),
            dma((M,)), dma((M,)),
            dma((N,)), dma((N,)),
            dma((N,)), dma((N,)),
            dma((M,)), dma((M,)),
        ],
        compiler_params=pltpu.CompilerParams(collective_id=0, has_side_effects=True),
    )(
        hidden_input_slots,
        base_weight.T,
        adapter_a.T,
        adapter_up_matrix,
        upstream.T,
        logp_new,
        logp_old,
        rewards,
        comp_lengths,
        assignment,
    )
    made = (projection, down, up, loss)
    kept = pl.pallas_call(
        keep,
        out_shape=tuple(jax.ShapeDtypeStruct(v.shape, v.dtype) for v in made),
        in_specs=[hbm] * 4,
        out_specs=(hbm,) * 4,
        scratch_shapes=[pltpu.VMEM(v.shape, v.dtype) for v in made] + [dma((4,)), dma((4,))],
    )(*made)
    projection, down, up, loss = kept
    return (projection.T, down.T, up, loss.reshape(1))


def solution(mesh):
    return jax.shard_map(
        on_device,
        mesh=mesh,
        in_specs=(
            P("group", None),
            P("group", "fsdp"),
            P("group", None),
            P(None, "fsdp"),
            P("group", "fsdp"),
            P("group", None, None),
            P("group", None, None),
            P("group", None),
            P("group", None),
            P("group", None),
        ),
        out_specs=(P("group", "fsdp"), P("group", None), P("group", "fsdp"), P("group")),
        check_vma=False,
    )
```

```python
import jax
import jax.numpy as jnp
from jax import lax
from jax.experimental import pallas as pl
from jax.experimental.pallas import tpu as pltpu
from jax.sharding import PartitionSpec as P

COMP = 16
ADAPTER_SCALING = 0.25
SPREAD_FLOOR = 0.16

N = 16
SIDE = 4
M = 16
TOP = 3
MESH = pl.DeviceIdType.MESH
ROWS = 308
SPLIT = 256
CUTS = ((0, 128), (128, 128))
REST = ROWS - SPLIT
Q_CUTS = ((SPLIT, 32), (SPLIT + 32, REST - 32))
F32 = jnp.float32
BF16 = jnp.bfloat16


def dot_nn(a, b):
    return lax.dot_general(a, b, (((1,), (0,)), ((), ())), preferred_element_type=F32)


def dot_nt(a, b):
    return lax.dot_general(a, b, (((1,), (1,)), ((), ())), preferred_element_type=F32)


def kernel(
    x_hbm, w_hbm, a_hbm, up_hbm, ups_hbm, new_hbm, old_hbm, rew_hbm, len_hbm, asg_hbm,
    proj_hbm, gdown_hbm, gup_hbm, loss_hbm,
    a_ref, up_ref, ups_ref, new_ref, old_ref, rew_ref, len_ref, asg_ref,
    proj_ref, gdown_ref, gup_ref, loss_ref, in_sem, out_sem,
    xv, wg, acc, up_p, upt, og, row, tab, hs, hr, ag_a, red, rs, zx, ag, lows, gus, gur, gds, gdr, gda,
    x_sem, h_s, h_r, a_s, a_r, zs, xs, fs, w_r, qx_s, qx_r, qz_s, qz_r, r_s, r_r, z_s, z_r, g_s, g_r, u_s, u_r, d_s, d_r, e_s, e_r,
):
    g = lax.axis_index("group")
    f = lax.axis_index("fsdp")
    z, x = lax.div(g, SIDE), lax.rem(g, SIDE)
    zh, i = lax.div(f, M), lax.rem(f, M)
    a, b = lax.div(i, SIDE), lax.rem(i, SIDE)
    hidden, cols = w_hbm.shape

    def copy(src, dst, ss, rr, tg, tf):
        return pltpu.make_async_remote_copy(
            src_ref=src, dst_ref=dst, send_sem=ss, recv_sem=rr,
            device_id=(tg, tf), device_id_type=MESH,
        )

    def each(fn, count=N):
        def body(d, carry):
            fn(d)
            return carry

        lax.fori_loop(1, count, body, 0)

    def group_to(d):
        return lax.rem(g + d, N)

    def group_from(d):
        return lax.rem(g + N - d, N)

    def side_to(d):
        return lax.rem(i + d, M)

    def side_from(d):
        return lax.rem(i + M - d, M)

    def top_to(d):
        return lax.rem(zh + d, TOP)

    def top_from(d):
        return lax.rem(zh + TOP - d, TOP)

    def gx(src, dst, ss, rr, d):
        return copy(src.at[group_to(d)], dst.at[g], ss.at[d], rr.at[d], group_to(d), f)

    def gx_in(src, dst, ss, rr, d):
        j = group_from(d)
        return copy(src.at[j], dst.at[j], ss.at[d], rr.at[d], j, f)

    def sx(src, dst, ss, rr, d):
        return copy(src.at[side_to(d)], dst.at[i], ss.at[d], rr.at[d], g, zh * M + side_to(d))

    def sx_in(src, dst, ss, rr, d):
        j = side_from(d)
        return copy(src.at[j], dst.at[j], ss.at[d], rr.at[d], g, zh * M + j)

    def sg(buf, ss, rr, d):
        return copy(buf.at[i], buf.at[i], ss.at[d], rr.at[d], g, zh * M + side_to(d))

    def sg_in(buf, ss, rr, d):
        j = side_from(d)
        return copy(buf.at[j], buf.at[j], ss.at[d], rr.at[d], g, zh * M + j)

    def tx(d):
        return copy(zx.at[zh], zx.at[zh], z_s.at[d], z_r.at[d], g, top_to(d) * M + i)

    def tx_in(d):
        j = top_from(d)
        return copy(zx.at[j], zx.at[j], z_s.at[d], z_r.at[d], g, j * M + i)

    barrier = pltpu.get_barrier_semaphore()

    def greet(d):
        pl.semaphore_signal(barrier, inc=1, device_id=(group_to(d), f), device_id_type=MESH)
        pl.semaphore_signal(barrier, inc=1, device_id=(g, zh * M + side_to(d)), device_id_type=MESH)

    each(greet)
    each(
        lambda d: pl.semaphore_signal(
            barrier, inc=1, device_id=(g, top_to(d) * M + i), device_id_type=MESH
        ),
        TOP,
    )

    small = [
        pltpu.make_async_copy(source, target, in_sem.at[at])
        for at, (source, target) in enumerate(
            (
                (rew_hbm, rew_ref), (asg_hbm, asg_ref), (len_hbm, len_ref), (old_hbm, old_ref),
                (new_hbm, new_ref), (up_hbm, up_ref), (a_hbm, a_ref), (ups_hbm, ups_ref),
                (w_hbm, wg.at[g]),
            )
        )
    ]
    for c in small:
        c.start()
    x_copy = pltpu.make_async_copy(x_hbm, xv, x_sem)
    x_copy.start()
    outs = [
        pltpu.make_async_copy(source, target, out_sem.at[at])
        for at, (source, target) in enumerate(
            (
                (loss_ref, loss_hbm), (gup_ref, gup_hbm),
                (gdown_ref, gdown_hbm), (proj_ref, proj_hbm),
            )
        )
    ]
    hs[...] = jnp.zeros(hs.shape, F32)
    up_p[...] = jnp.zeros(up_p.shape, BF16)
    og[...] = jnp.zeros(og.shape, BF16)
    for c in small:
        c.wait()

    rewards = rew_ref[...]
    mean = jnp.sum(rewards, axis=1, keepdims=True) / COMP
    var = jnp.sum(rewards * rewards, axis=1, keepdims=True) / COMP - mean * mean
    spread = jnp.sqrt(jnp.maximum(var, SPREAD_FLOOR))
    advantage = (rewards - mean) / spread
    dest = asg_ref[...] == lax.broadcasted_iota(jnp.int32, (N, N), 0)
    lengths = len_ref[...].astype(F32)
    old = old_ref[0]
    sent_old = jnp.zeros((N, N), F32)
    for k in range(N):
        sent_old = jnp.where(dest[:, k : k + 1], old[k : k + 1, :], sent_old)
    sent_adv = jnp.sum(jnp.where(dest, advantage, 0.0), axis=1, keepdims=True)
    sent_len = jnp.sum(jnp.where(dest, lengths, 0.0), axis=1, keepdims=True)
    for at, value in enumerate((sent_old, sent_adv, sent_len)):
        tab[...] = jnp.zeros(tab.shape, F32)
        tab[:, 0:N] = jnp.broadcast_to(value, (N, N))
        rolled = pltpu.roll(tab[...], g * N, axis=1)
        for t in range(N):
            hs[t, at : at + 1, :] = rolled[t : t + 1, :]
    hr[g] = hs[g]
    for j in range(N):
        row[0:1, j * N : (j + 1) * N] = new_ref[0, j : j + 1, :]

    up_p[:, 0:hidden] = up_ref[...]
    upt[...] = up_p[...].astype(F32).T.astype(BF16)

    pl.semaphore_wait(barrier, 2 * (N - 1) + TOP - 1)

    quarter = pl.ds(pl.multiple_of(b * 128, 128), 128)

    def ax(d):
        return copy(
            a_ref.at[:, quarter], ag_a.at[z], a_s.at[d], a_r.at[z], group_to(d), f
        )

    gives = (x == a) & (z - 1 + lax.div(SIDE - z, SIDE) == zh)
    @pl.when(x == a)
    def _():
        ag_a[z] = a_ref[:, quarter]

    @pl.when(gives)
    def _():
        each(lambda d: ax(d).start())

    each(lambda d: gx(hs, hr, h_s, h_r, d).start())

    right = z * SIDE + lax.rem(x + 1, SIDE)
    left = z * SIDE + lax.rem(x + SIDE - 1, SIDE)

    def part(s, h):
        return wg.at[s, pl.ds(*CUTS[h]), :]

    def wx(s, h, sem, tg):
        return copy(part(s, h), part(s, h), sem, w_r.at[s, h], tg, f)

    def arrive(s, h):
        wx(s, h, fs.at[0, 0], g).wait_recv()

    near = [z, z + 1 - 2 * lax.rem(z, 2), 2 - lax.div(z, 2), 3 - 3 * lax.div(z, 2)]
    inner = (z == 1) | (z == 2)
    outer = (z == 0) | (z == 3)
    beyond = [None, 3 - z, 3 * (z - 1), 3 * (z - 1)]

    def z_first(go):
        for h in (0, 1):

            @pl.when(z < SIDE - 1)
            def _():
                go(wx(g, h, zs.at[0, h], g + SIDE))

            @pl.when(z > 0)
            def _():
                go(wx(g, h, zs.at[4, h], g - SIDE))

    def z_next(k, go):
        for h in (0, 1):
            go(wx(near[k] * SIDE + x, h, zs.at[k, h], beyond[k] * SIDE + x))

    def x_send(k, go):
        s = near[k] * SIDE + x
        go(wx(s, 0, xs.at[k, 0, 0], right))
        go(wx(s, 1, xs.at[k, 1, 1], left))
        go(wx(s, 1, xs.at[k, 0, 1], right))
        go(wx(s, 0, xs.at[k, 1, 0], left))

    def shard(k, off):
        return near[k] * SIDE + lax.rem(x + off, SIDE)

    def x_pass(k, go):
        go(wx(shard(k, 3), 0, fs.at[k, 0], right))
        go(wx(shard(k, 1), 1, fs.at[k, 1], left))

    def start(c):
        c.start()

    def done(c):
        c.wait_send()

    def pass_on(k):
        arrive(shard(k, 3), 0)
        arrive(shard(k, 1), 1)
        x_pass(k, start)

    def land(k):
        arrive(near[k] * SIDE + x, 0)
        arrive(near[k] * SIDE + x, 1)

    def q_copy(ref, sem, rem, tg):
        return copy(ref, ref, sem, rem, tg, f)

    def q_part(s):
        return wg.at[s, pl.ds(SPLIT, REST), :]

    def q_half(s, h):
        return wg.at[s, pl.ds(*Q_CUTS[h]), :]

    def q_rows(zz, e):
        return wg.at[pl.ds(zz * SIDE + 2 * e, 2), pl.ds(SPLIT, REST), :]

    def q_send(go):
        go(q_copy(q_part(g), qx_s.at[0], qx_r.at[0], right))
        go(q_copy(q_part(g), qx_s.at[1], qx_r.at[1], left))

    def q_pass(go):
        go(q_copy(q_half(shard(0, 3), 0), qx_s.at[2], qx_r.at[2], right))
        go(q_copy(q_half(shard(0, 1), 1), qx_s.at[3], qx_r.at[3], left))

    def q_first(go):
        for e in (0, 1):

            @pl.when(z < SIDE - 1)
            def _():
                go(q_copy(q_rows(z, e), qz_s.at[0, e], qz_r.at[z, e], g + SIDE))

            @pl.when(z > 0)
            def _():
                go(q_copy(q_rows(z, e), qz_s.at[4, e], qz_r.at[z, e], g - SIDE))

    def q_next(k, e, go):
        tg = beyond[k] * SIDE + x
        go(q_copy(q_rows(near[k], e), qz_s.at[k, e], qz_r.at[near[k], e], tg))

    def q_land(k, e):
        q_copy(q_rows(near[k], e), qz_s.at[0, e], qz_r.at[near[k], e], g).wait_recv()

    def q_relay(k):
        @pl.when(inner)
        def _():
            for e in (0, 1):
                q_land(k, e)
                q_next(k, e, start)

    def x_block(s):
        return xv[:, pl.ds(pl.multiple_of(s * cols, cols), cols)]

    def multiply(s, first=False):
        piece = dot_nt(wg[s, 0:SPLIT, :], x_block(s))
        if first:
            acc[0:SPLIT, :] = piece
        else:
            acc[0:SPLIT, :] += piece

    def q_multiply(k, first=False):
        piece = None
        for off in range(SIDE):
            s = near[k] * SIDE + off
            term = dot_nt(wg[s, SPLIT:ROWS, :], x_block(s))
            piece = term if piece is None else piece + term
        if first:
            acc[SPLIT:ROWS, :] = piece
        else:
            acc[SPLIT:ROWS, :] += piece

    def finish(k):
        arrive(shard(k, 3), 1)
        multiply(shard(k, 3))
        arrive(shard(k, 1), 0)
        multiply(shard(k, 1))
        arrive(shard(k, 2), 0)
        arrive(shard(k, 2), 1)
        multiply(shard(k, 2))

    q_send(start)
    z_first(start)
    x_send(0, start)

    q_copy(q_part(shard(0, 3)), qx_s.at[0], qx_r.at[0], g).wait_recv()
    q_copy(q_part(shard(0, 1)), qx_s.at[0], qx_r.at[1], g).wait_recv()
    q_pass(start)
    pass_on(0)
    land(1)

    @pl.when(inner)
    def _():
        z_next(1, start)

    x_send(1, start)

    @pl.when(inner)
    def _():
        land(2)
        z_next(2, start)
        x_send(2, start)

    each(lambda d: gx_in(hs, hr, h_s, h_r, d).wait_recv())
    got = hr[0]
    for j in range(1, N):
        got = got + hr[j]
    recv_old, recv_adv, recv_len = got[0:1, :], got[1:2, :], got[2:3, :]
    position = lax.rem(lax.broadcasted_iota(jnp.int32, (1, N * N), 1), N).astype(F32)
    ratio = jnp.exp(row[0:1, :] - recv_old)
    coef = jnp.where(position < recv_len, -(recv_adv * ratio) / (recv_len * COMP), 0.0)
    loss_ref[...] = jnp.sum(coef, axis=1, keepdims=True)
    outs[0].start()
    og[0:hidden, :] = (coef * ups_ref[...].astype(F32)).astype(BF16)
    back = dot_nn(up_p[...], og[...])
    for p in range(M):
        red[p, 4:8, :] = back[p * 4 : (p + 1) * 4, :]


    def adapter(q, at_first):
        @pl.when((x != a) | (z != q))
        def _():
            copy(
                a_ref.at[:, quarter], ag_a.at[q], a_s.at[0], a_r.at[q], g, f
            ).wait_recv()

        at = (q * SIDE + a) * cols + b * 128
        term = dot_nt(ag_a[q], xv[:, pl.ds(pl.multiple_of(at, 128), 128)])
        if at_first:
            lows[...] = term
        else:
            lows[...] += term

    x_copy.wait()
    adapter(zh + 1, True)

    @pl.when(zh == 0)
    def _():
        adapter(0, False)

    low = lows[...]
    for p in range(M):
        red[p, 0:4, :] = low[p * 4 : (p + 1) * 4, :]
    rs[i] = red[i]
    each(lambda d: sx(red, rs, r_s, r_r, d).start())

    q_copy(q_half(shard(0, 2), 0), qx_s.at[0], qx_r.at[2], g).wait_recv()
    q_copy(q_half(shard(0, 2), 1), qx_s.at[0], qx_r.at[3], g).wait_recv()

    @pl.when(outer)
    def _():
        q_first(start)

    multiply(g, first=True)

    @pl.when(inner)
    def _():
        land(3)
        z_next(3, start)

    @pl.when(outer)
    def _():
        land(2)
        x_send(2, start)

    each(lambda d: sx_in(red, rs, r_s, r_r, d).wait_recv())
    total = rs[0]
    for j in range(1, M):
        total = total + rs[j]
    zx[zh] = total
    each(lambda d: tx(d).start(), TOP)

    @pl.when(inner)
    def _():
        q_first(start)

    pass_on(1)
    q_relay(1)

    each(lambda d: tx_in(d).wait_recv(), TOP)
    whole = zx[0] + zx[1] + zx[2]
    ag[i] = whole[0:4, :].astype(BF16).astype(F32)
    each(lambda d: sg(ag, g_s, g_r, d).start())
    bl = whole.astype(BF16)

    def down(t, carry):
        for u in range(SIDE):
            full = ADAPTER_SCALING * dot_nn(bl, x_block(t * SIDE + u))
            gds[t * SIDE + u] = full[4:8, :]
        return carry

    lax.fori_loop(0, SIDE, down, 0)
    gdr[g] = gds[g]
    each(lambda d: gx(gds, gdr, d_s, d_r, d).start())

    pass_on(2)

    @pl.when(outer)
    def _():
        land(3)

    x_send(3, start)
    q_relay(2)
    finish(0)
    multiply(shard(1, 0))

    each(lambda d: sg_in(ag, g_s, g_r, d).wait_recv())
    for j in range(M):
        lows[j * 4 : (j + 1) * 4, :] = ag[j]
    low_b = lows[...].astype(BF16)
    gp = ADAPTER_SCALING * dot_nt(low_b, og[...])
    for t in range(N):
        gus[t] = gp[t * 4 : (t + 1) * 4, :]
    gur[g] = gus[g]
    each(lambda d: gx(gus, gur, u_s, u_r, d).start())

    q_relay(3)

    each(lambda d: gx(hs, hr, h_s, h_r, d).wait_send())

    @pl.when(gives)
    def _():
        each(lambda d: ax(d).wait_send())

    q_send(done)
    q_pass(done)
    z_first(done)

    @pl.when(inner)
    def _():
        for k in range(1, SIDE):
            z_next(k, done)

    for k in (0, 1):
        x_send(k, done)
        x_pass(k, done)
    each(lambda d: sx(red, rs, r_s, r_r, d).wait_send())
    each(lambda d: tx(d).wait_send(), TOP)
    pass_on(3)

    each(lambda d: gx_in(gds, gdr, d_s, d_r, d).wait_recv())
    total_down = gdr[0]
    for j in range(1, N):
        total_down = total_down + gdr[j]
    gda[i] = total_down
    each(lambda d: sg(gda, e_s, e_r, d).start())

    q_multiply(0, first=True)
    acc[...] += ADAPTER_SCALING * dot_nn(upt[0:ROWS, :], low_b)
    finish(1)
    multiply(shard(2, 0))
    finish(2)
    multiply(shard(3, 0))
    for k in (1, 2):

        @pl.when(outer)
        def _():
            q_land(k, 0)
            q_land(k, 1)

        q_multiply(k)

    each(lambda d: gx_in(gus, gur, u_s, u_r, d).wait_recv())
    total_up = gur[0]
    for j in range(1, N):
        total_up = total_up + gur[j]
    gup_ref[...] = total_up[:, 0:hidden]
    outs[1].start()

    q_first(done)

    @pl.when(inner)
    def _():
        for e in (0, 1):
            q_next(1, e, done)

    x_send(2, done)
    x_pass(2, done)
    each(lambda d: sg(ag, g_s, g_r, d).wait_send())
    each(lambda d: gx(gds, gdr, d_s, d_r, d).wait_send())
    each(lambda d: gx(gus, gur, u_s, u_r, d).wait_send())

    @pl.when(outer)
    def _():
        q_land(3, 0)
        q_land(3, 1)

    q_multiply(3)
    each(lambda d: sg_in(gda, e_s, e_r, d).wait_recv())
    for j in range(M):
        gdown_ref[j * 4 : (j + 1) * 4, :] = gda[j]
    outs[2].start()
    finish(3)
    proj_ref[...] = acc[...].astype(BF16)
    outs[3].start()

    @pl.when(inner)
    def _():
        for k in (2, 3):
            for e in (0, 1):
                q_next(k, e, done)

    x_send(3, done)
    x_pass(3, done)
    each(lambda d: sg(gda, e_s, e_r, d).wait_send())
    for c in outs:
        c.wait()


def keep(*refs):
    given, taken, held, come, go = refs[:4], refs[4:8], refs[8:12], refs[12], refs[13]
    loads = [pltpu.make_async_copy(given[n], held[n], come.at[n]) for n in range(4)]
    stores = [pltpu.make_async_copy(held[n], taken[n], go.at[n]) for n in range(4)]
    for c in loads:
        c.start()
    for load, store in zip(loads, stores):
        load.wait()
        store.start()
    for c in stores:
        c.wait()


def on_device(
    hidden_input_slots,
    base_weight,
    adapter_a,
    adapter_up_matrix,
    upstream,
    logp_new,
    logp_old,
    rewards,
    comp_lengths,
    assignment,
):
    tokens, depth = hidden_input_slots.shape
    share, hidden = base_weight.shape
    rank = adapter_a.shape[1]
    hbm = pl.BlockSpec(memory_space=pl.ANY)
    dma = pltpu.SemaphoreType.DMA
    projection, down, up, loss = pl.pallas_call(
        kernel,
        out_shape=(
            jax.ShapeDtypeStruct((hidden, tokens), BF16),
            jax.ShapeDtypeStruct((rank, share), F32),
            jax.ShapeDtypeStruct((rank // N, hidden), F32),
            jax.ShapeDtypeStruct((1, 1), F32),
        ),
        in_specs=[hbm] * 10,
        out_specs=(hbm,) * 4,
        scratch_shapes=[
            pltpu.VMEM((rank, share), BF16),
            pltpu.VMEM((rank, hidden), BF16),
            pltpu.VMEM((hidden, tokens), BF16),
            pltpu.VMEM(logp_new.shape, F32),
            pltpu.VMEM(logp_old.shape, F32),
            pltpu.VMEM(rewards.shape, F32),
            pltpu.VMEM(comp_lengths.shape, jnp.int32),
            pltpu.VMEM(assignment.shape, jnp.int32),
            pltpu.VMEM((hidden, tokens), BF16),
            pltpu.VMEM((rank, share), F32),
            pltpu.VMEM((rank // N, hidden), F32),
            pltpu.VMEM((1, 1), F32),
            dma((9,)),
            dma((4,)),
            pltpu.VMEM((tokens, depth), BF16),
            pltpu.VMEM((N, ROWS, share), BF16),
            pltpu.VMEM((ROWS, tokens), F32),
            pltpu.VMEM((rank, 384), BF16),
            pltpu.VMEM((384, rank), BF16),
            pltpu.VMEM((384, tokens), BF16),
            pltpu.VMEM((8, tokens), F32),
            pltpu.VMEM((N, tokens), F32),
            pltpu.VMEM((N, 4, tokens), F32),
            pltpu.VMEM((N, 4, tokens), F32),
            pltpu.VMEM((SIDE, rank, 128), BF16),
            pltpu.VMEM((M, 8, tokens), F32),
            pltpu.VMEM((M, 8, tokens), F32),
            pltpu.VMEM((TOP, 8, tokens), F32),
            pltpu.VMEM((M, 4, tokens), F32),
            pltpu.VMEM((rank, tokens), F32),
            pltpu.VMEM((N, 4, 384), F32),
            pltpu.VMEM((N, 4, 384), F32),
            pltpu.VMEM((N, 4, share), F32),
            pltpu.VMEM((N, 4, share), F32),
            pltpu.VMEM((M, 4, share), F32),
            dma,
            dma((N,)), dma((N,)),
            dma((N,)), dma((SIDE,)),
            dma((5, 2)), dma((SIDE, 2, 2)), dma((SIDE, 2)), dma((N, 2)),
            dma((4,)), dma((4,)), dma((5, 2)), dma((SIDE, 2)),
            dma((M,)), dma((M,)),
            dma((TOP,)), dma((TOP,)),
            dma((M,)), dma((M,)),
            dma((N,)), dma((N,)),
            dma((N,)), dma((N,)),
            dma((M,)), dma((M,)),
        ],
        compiler_params=pltpu.CompilerParams(collective_id=0, has_side_effects=True),
    )(
        hidden_input_slots,
        base_weight.T,
        adapter_a.T,
        adapter_up_matrix,
        upstream.T,
        logp_new,
        logp_old,
        rewards,
        comp_lengths,
        assignment,
    )
    made = (projection, down, up, loss)
    kept = pl.pallas_call(
        keep,
        out_shape=tuple(jax.ShapeDtypeStruct(v.shape, v.dtype) for v in made),
        in_specs=[hbm] * 4,
        out_specs=(hbm,) * 4,
        scratch_shapes=[pltpu.VMEM(v.shape, v.dtype) for v in made] + [dma((4,)), dma((4,))],
    )(*made)
    projection, down, up, loss = kept
    return (projection.T, down.T, up, loss.reshape(1))


def solution(mesh):
    return jax.shard_map(
        on_device,
        mesh=mesh,
        in_specs=(
            P("group", None),
            P("group", "fsdp"),
            P("group", None),
            P(None, "fsdp"),
            P("group", "fsdp"),
            P("group", None, None),
            P("group", None, None),
            P("group", None),
            P("group", None),
            P("group", None),
        ),
        out_specs=(P("group", "fsdp"), P("group", None), P("group", "fsdp"), P("group")),
        check_vma=False,
    )
```
